512 devices in a mesh: panel: 2 (over x_hi), rad: 8 (over z), ang: 32 (over y, x_lo, core).
Axes of the slice: x: 4 (x_hi: 2, x_lo: 2; x = x_hi * 2 + x_lo), y: 8, z: 8, core: 2. Of those that a mesh axis runs over, the one named last changes fastest.
Arguments:
- adj_final: float32 [2, 7, 8, 256, 1536], P('panel', None, 'rad', 'ang'), may hold values from -6 to 6
- cond: float32 [2, 8, 256, 1536], P('panel', 'rad', 'ang'), may hold values from 0.5 to 1.5
- diffus: float32 [7], replicated, may hold values from 0.02 to 0.1
- couple: float32 [7, 7], replicated, may hold values from -0.1 to 0.1
- ghost_row: int32 [2, 4, 256], replicated, may hold values from 0 to 255
- ghost_col: int32 [2, 4, 256], replicated, may hold values from 0 to 1535
- ghost_wt: float32 [2, 4, 256], replicated, may hold values from 0.5 to 1.5
- obs_dest: int32 [2, 8, 8192, 1], P('panel', 'rad', 'ang'), may hold values from 0 to 31; in each aligned block of 256 rows (0 to 255, 256 to 511, ..., all dimensions but the last counted through in order) at most 16 rows name the same one
- obs_cell: int32 [2, 8, 4, 8192], P('panel', 'rad', None, 'ang'), may hold values from 0 to 12287
- obs_wt: float32 [2, 8, 4, 8192], P('panel', 'rad', None, 'ang'), may hold values from 0.2 to 1
- misfit: float32 [2, 8, 2, 8192], P('panel', 'rad', None, 'ang'), may hold values from -6 to 6
Outputs:
- adj_start: float32 [2, 7, 8, 256, 1536], P('panel', None, 'rad', 'ang')
The draws below stay inside these ranges and needn't reach their ends.
Inputs may be any that keep to these rules, and one draw needn't show every extreme that they name: `obs_dest`: owner tile, within the observation's own panel, whose outermost layer holds it; among the 256 observations of one device at most 16 name one owner. `obs_cell`: row within the owner's tile times 1536 plus column.
All inputs are finite; a program needn't handle non-finite values.
Results may differ from the reference program's by a relative error of at most 0.000088.
Values sent between devices are 32-bit elements; how exact they have to be, the bound alone decides.
A program may use at most 64 MiB of HBM per device.

```python
import math
import jax
import jax.numpy as jnp
import numpy as np
from jax import lax

FIELDS = 7
TH_DEV = 8
PH = 1536
OBS_DEV = 256
TILES = 32
RGROUPS = 8
NR = 8
NT = 256
NOBS = 8192
CAP = 16


def touch_ends(drawn, stream_key, smallest, high):
    longest = drawn.shape.index(max(drawn.shape))
    spots = []
    for shift in (0, 1):
        where = [jax.random.randint(jax.random.fold_in(stream_key, axis), (), 0, length) for axis, length in enumerate(drawn.shape)]
        where[longest] = (where[longest] + shift) % drawn.shape[longest]
        spots.append(tuple(where))
    return drawn.at[spots[0]].set(smallest).at[spots[1]].set(high)


def block_levels(key, dims, shards, smallest, high):
    factor_of = 1.0
    for position, parts in shards:
        steps = jax.random.uniform(jax.random.fold_in(jax.random.fold_in(key, 6), position), (parts,), jnp.float32, smallest / len(shards), high / len(shards))
        factor_of = factor_of * jnp.repeat(jnp.exp(steps), dims[position] // parts).reshape((-1,) + (1,) * (len(dims) - 1 - position))
    return factor_of


def routed_block(rng, own, number, rows, count, top, limit, slope):
    sequence = jax.random.permutation(rng, count)
    packed, usual = portions_of(count, rows * top, limit, slope, True), portions_of(count, rows * top, limit, slope, False)
    places = jnp.arange(count)

    def named(tallies, rotation):
        used = int((tallies > 0).sum())
        fixed = max(1, used // 4)
        moved = fixed + (places - fixed + rotation * (used - fixed)) % max(1, count - fixed)
        return jnp.zeros((count,), jnp.int32).at[sequence[jnp.where(places < fixed, places, moved)]].set(jnp.asarray(tallies, jnp.int32))

    tallies = jnp.where(number % 4 == 0, named(packed, number // 4), named(usual, number - number // 4 - 1))
    mixed = jax.random.permutation(jax.random.fold_in(own, 3), count)
    giver, sink = mixed[0:count // 2 * 2:2], mixed[1:count // 2 * 2:2]
    margin = jnp.minimum(tallies[giver] - 1, limit - tallies[sink]) // 2
    margin = jnp.where((giver == sequence[0]) | (sink == sequence[0]) | (tallies[sink] == 0), 0, jnp.maximum(margin, 0))
    moved = jax.random.randint(jax.random.fold_in(own, 4), (count // 2,), 0, 1 << 20) % (margin + 1)
    tallies = tallies.at[giver].add(-moved).at[sink].add(moved)
    labels = jnp.searchsorted(jnp.cumsum(tallies), jnp.arange(rows * top), side="right").astype(jnp.int32)
    grid = labels.reshape(top, rows).T
    grid = grid[jax.random.permutation(jax.random.fold_in(own, 1), rows)]
    rotation = jax.random.randint(jax.random.fold_in(own, 2), (rows, 1), 0, top)
    return jnp.take_along_axis(grid, (jnp.arange(top)[None, :] + rotation) % top, axis=1)


def portions_of(amount, total, reach, skew, full):
    portions = [(1 << 20) // math.isqrt(standing ** skew) + 1 for standing in range(1, amount + 1)]
    largest = reach if full else min(reach, max(-(-total // amount), total * portions[0] // sum(portions)))
    least = 1 if total - largest >= amount - 1 else 0
    holding, rest = [largest] + [least] * (amount - 1), total - largest - least * (amount - 1)
    while rest > 0:
        free = [i for i in range(1, amount) if holding[i] < largest] or [i for i in range(1, amount) if holding[i] < reach]
        pool, remaining = sum([portions[i] for i in free]), rest
        for i in free:
            addition = min(reach - holding[i], max(1, remaining * portions[i] // pool), rest)
            holding[i] = holding[i] + addition
            rest = rest - addition
    return np.array(holding)


def noise(stream_key, extent, scale, limit, cuts=(), dtype=jnp.bfloat16):
    loudness = block_levels(stream_key, extent, cuts, -0.22, 0.18) if cuts else 1.0
    values = jax.random.normal(stream_key, extent, jnp.float32) * scale * loudness
    return jnp.minimum(jnp.maximum(values, -limit), limit).astype(dtype)


def setup_inputs(seed: int = 0) -> dict:
    splits = jax.random.split(jax.random.key(seed), 12)
    adj_final = noise(splits[0], (2, FIELDS, NR, NT, PH), 1.0, 6.0, ((0, 2), (2, 8), (3, 32)), jnp.float32)
    cond = jnp.clip(jnp.exp(math.log(1.5) - 1.0986123 * jax.random.uniform(splits[1], (2, NR, NT, PH), jnp.float32) ** block_levels(splits[1], (2, NR, NT, PH), ((0, 2), (1, 8), (2, 32)), -0.2, 0.2)), 0.5, 1.5)
    diffus = jnp.clip(jnp.exp(jax.random.uniform(splits[2], (FIELDS,), jnp.float32, math.log(0.02), math.log(0.1))), 0.02, 0.1)
    couple = jnp.clip(jax.random.uniform(splits[3], (FIELDS, FIELDS), jnp.float32, -0.1, 0.1), -0.1, 0.1)
    ghost_row = touch_ends(jax.random.randint(splits[4], (2, 4, NT), 0, NT), jax.random.fold_in(splits[4], 1), 0, NT - 1).astype(jnp.int32)
    ghost_col = touch_ends(jax.random.randint(splits[5], (2, 4, NT), 0, PH), jax.random.fold_in(splits[5], 1), 0, PH - 1).astype(jnp.int32)
    ghost_wt = jnp.clip(jax.random.uniform(splits[6], (2, 4, NT), jnp.float32, 0.5, 1.5), 0.5, 1.5)
    obs_dest_keys = jax.random.split(jax.random.fold_in(splits[7], 1), 2 * RGROUPS * NOBS // OBS_DEV)
    obs_dest_turns = jax.random.permutation(jax.random.fold_in(splits[7], 3), 2 * RGROUPS * NOBS // OBS_DEV)
    obs_dest = jax.vmap(lambda own, number: routed_block(jax.random.fold_in(splits[7], 2), own, number, OBS_DEV, TILES, 1, CAP, 2))(obs_dest_keys, obs_dest_turns).reshape((2, RGROUPS, NOBS, 1))
    obs_cell = touch_ends(jax.random.randint(splits[8], (2, RGROUPS, 4, NOBS), 0, TH_DEV * PH), jax.random.fold_in(splits[8], 1), 0, (TH_DEV * PH) - 1).astype(jnp.int32)
    obs_wt = jnp.clip(0.2 + 0.8 * jax.random.uniform(splits[9], (2, RGROUPS, 4, NOBS), jnp.float32) ** block_levels(splits[9], (2, RGROUPS, 4, NOBS), ((0, 2), (1, 8), (3, 32)), -0.2, 0.2), 0.2, 1.0)
    misfit = noise(splits[10], (2, RGROUPS, 2, NOBS), 1.0, 6.0, ((0, 2), (1, 8), (3, 32)), jnp.float32)
    return dict(adj_final=adj_final, cond=cond, diffus=diffus, couple=couple, ghost_row=ghost_row, ghost_col=ghost_col, ghost_wt=ghost_wt, obs_dest=obs_dest, obs_cell=obs_cell, obs_wt=obs_wt, misfit=misfit)


def laplace(scaled):
    padded = jnp.pad(scaled, ((0, 0), (0, 0), (1, 1), (1, 1), (1, 1)))
    total = padded[:, :, 2:, 1:-1, 1:-1] + padded[:, :, :-2, 1:-1, 1:-1]
    total = total + padded[:, :, 1:-1, 2:, 1:-1] + padded[:, :, 1:-1, :-2, 1:-1]
    total = total + padded[:, :, 1:-1, 1:-1, 2:] + padded[:, :, 1:-1, 1:-1, :-2]
    return total - 6.0 * scaled


def ghost_panel(other, ghost_row, ghost_col, ghost_wt):
    fields, layers, rows, columns = other.shape
    edges = jnp.stack([other[..., 0], other[..., -1]], axis=2)
    values = edges[:, :, :, None, :] * ghost_wt[None, None]
    flat_index = (ghost_row * columns + ghost_col).reshape(-1)
    target = jnp.zeros((fields, layers, rows * columns), jnp.float32)
    target = target.at[:, :, flat_index].add(values.reshape(fields, layers, -1))
    return target.reshape(fields, layers, rows, columns)


def surface_forcing(obs_dest, obs_cell, obs_wt, misfit):
    panels = []
    for panel_index in range(2):
        owners = obs_dest[panel_index, :, :, 0]
        cells = obs_cell[panel_index]
        row_index = owners[:, None, :] * TH_DEV + cells // PH
        flat_index = row_index * PH + cells % PH
        values = misfit[panel_index][:, :, None, :] * obs_wt[panel_index][:, None, :, :]
        values = jnp.transpose(values, (1, 0, 2, 3)).reshape(2, -1)
        target = jnp.zeros((2, NT * PH), jnp.float32)
        target = target.at[:, flat_index.reshape(-1)].add(values)
        panels.append(target)
    return jnp.stack(panels)


def adjoint_step(adjoint, coeff, couple, ghost_row, ghost_col, ghost_wt, source):
    scaled = coeff * adjoint
    lap = laplace(scaled)
    ghost = jnp.stack([ghost_panel(scaled[1], ghost_row, ghost_col, ghost_wt),
                       ghost_panel(scaled[0], ghost_row, ghost_col, ghost_wt)])
    coupled = jnp.einsum("ec,pelrk->pclrk", couple, adjoint, precision=lax.Precision.HIGHEST)
    updated = adjoint + lap + ghost + coupled
    return updated.at[:, 3, NR - 1].add(source)


def reference(adj_final, cond, diffus, couple, ghost_row, ghost_col, ghost_wt, obs_dest, obs_cell, obs_wt, misfit):
    forcing = surface_forcing(obs_dest, obs_cell, obs_wt, misfit)
    coeff = diffus[None, :, None, None, None] * cond[:, None]
    first = adjoint_step(adj_final, coeff, couple, ghost_row, ghost_col, ghost_wt,
                         forcing[:, 1].reshape(2, NT, PH))
    return adjoint_step(first, coeff, couple, ghost_row, ghost_col, ghost_wt,
                        forcing[:, 0].reshape(2, NT, PH))
```

```python
import functools
import jax
import jax.numpy as jnp
from jax import lax
from jax.experimental import pallas as pl
from jax.experimental.pallas import tpu as pltpu
from jax.sharding import PartitionSpec as P

MESH = pl.DeviceIdType.MESH
F32, BF16 = jnp.float32, jnp.bfloat16
FIELDS, ROWS, COLS = 7, 8, 1536
LANES = 128
BLOCKS = COLS // LANES
HIGH = ROWS * BLOCKS
LAYERS, TILES, GROUP = 8, 32, 4
LINES = TILES // GROUP
SLOTS = 16
POINTS = 4
OBS = 256
EDGE = TILES * ROWS
FORCED = 3

PIECES = ((0, 1), (11, 12), (1, 3), (3, 5), (5, 7), (7, 9), (9, 11))
GROUPS = ((0, 1), (2,), (3,), (4,), (5,), (6,))
ROW_PIECES = (((0, 12),), ((0, 1), (11, 12), (1, 5), (5, 9), (9, 11)))
ROW_AFTER = {0: (0, 1), 2: (2,), 4: (3,), 5: (4,)}


def iota(shape, dim, dtype=jnp.int32):
    value = lax.broadcasted_iota(jnp.int32, shape, dim)
    return value if dtype == jnp.int32 else value.astype(dtype)


def dot_rows(a, b, precision=None):
    return lax.dot_general(
        a, b, (((1,), (1,)), ((), ())), precision=precision, preferred_element_type=F32
    )


def two_parts(row):
    wide = jnp.broadcast_to(row, (16, row.shape[1]))
    high = wide.astype(BF16)
    low = (wide - high.astype(F32)).astype(BF16)
    return high, low


def spread(onehot_high, row):
    count, width = onehot_high.shape
    grid = onehot_high.reshape(count // 16, 16, width)
    return [(grid * part[None]).reshape(count, width) for part in two_parts(row)]


def kernel(
    adj, cond, diffus, couple, ghost_row, ghost_col, ghost_wt, dest, cell, obs_wt, misfit,
    out,
    scaled_a, scaled_b, base, layer_in, row_out, row_in,
    edge_out, edge_in, edge_sum, edge_all, edge_rows,
    high_hot, low_hot,
    outbox, line_in, pair_sum, tile_in, forced_in, forcing,
    layer_ss, layer_rs, row_ss, row_rs,
    edge_ss, edge_rs, line_ss, line_rs,
    obs1_ss, obs1_rs, obs2_ss, obs2_rs, obs3_ss, obs3_rs,
):
    p, z, a = lax.axis_index("panel"), lax.axis_index("rad"), lax.axis_index("ang")
    y, q = a // GROUP, lax.rem(a, GROUP)
    has_low, has_high = z > 0, z < LAYERS - 1
    has_north, has_south = a > 0, a < TILES - 1
    outer = z == LAYERS - 1
    inner = z < LAYERS - 1
    scaled = (scaled_a, scaled_b)

    def along_line(step):
        return lax.rem(y + step, LINES)

    def beside(step):
        return lax.rem(q + step, GROUP)

    barrier = pltpu.get_barrier_semaphore()

    def greet(panel, layer, tile):
        pl.semaphore_signal(barrier, inc=1, device_id=(panel, layer, tile), device_id_type=MESH)

    @pl.when(has_low)
    def _():
        greet(p, z - 1, a)

    @pl.when(has_high)
    def _():
        greet(p, z + 1, a)

    @pl.when(has_north)
    def _():
        greet(p, z, a - 1)

    @pl.when(has_south)
    def _():
        greet(p, z, a + 1)

    for i in range(GROUP):
        greet(1 - p, z, y * GROUP + i)
    for i in range(1, LINES):
        greet(p, z, along_line(i) * GROUP + q)
    for i in range(1, GROUP):
        greet(p, z, y * GROUP + beside(i))

    @pl.when(outer)
    def _():
        for i in range(LAYERS - 1):
            greet(p, i, a)

    def layer_copy(step, way, piece):
        start, stop = PIECES[piece]
        cols = slice(start * LANES, stop * LANES)
        return pltpu.make_async_remote_copy(
            src_ref=scaled[step].at[:, :, cols],
            dst_ref=layer_in.at[step, way, :, :, cols],
            send_sem=layer_ss.at[step, way, piece],
            recv_sem=layer_rs.at[step, way, piece],
            device_id=(p, z + 1 if way == 0 else z - 1, a),
            device_id_type=MESH,
        )

    def row_copy(step, way, piece):
        start, stop = ROW_PIECES[step][piece]
        cols = slice(start * LANES, stop * LANES)
        return pltpu.make_async_remote_copy(
            src_ref=row_out.at[step, way, :, cols],
            dst_ref=row_in.at[step, way, :, cols],
            send_sem=row_ss.at[step, way, piece],
            recv_sem=row_rs.at[step, way, piece],
            device_id=(p, z, a + 1 if way == 0 else a - 1),
            device_id_type=MESH,
        )

    def edge_copy(step, i, origin):
        return pltpu.make_async_remote_copy(
            src_ref=edge_out.at[step],
            dst_ref=edge_in.at[step, origin],
            send_sem=edge_ss.at[step, i],
            recv_sem=edge_rs.at[step, origin],
            device_id=(1 - p, z, y * GROUP + i),
            device_id_type=MESH,
        )

    def line_copy(step, i, origin):
        return pltpu.make_async_remote_copy(
            src_ref=edge_sum.at[step],
            dst_ref=edge_all.at[step, origin],
            send_sem=line_ss.at[step, i],
            recv_sem=line_rs.at[step, origin],
            device_id=(p, z, along_line(i) * GROUP + q),
            device_id_type=MESH,
        )

    def obs1_copy(i, origin):
        target = along_line(i)
        return pltpu.make_async_remote_copy(
            src_ref=outbox.at[pl.ds(target * GROUP, GROUP)],
            dst_ref=line_in.at[origin],
            send_sem=obs1_ss.at[i],
            recv_sem=obs1_rs.at[origin],
            device_id=(p, z, target * GROUP + q),
            device_id_type=MESH,
        )

    def obs2_copy(i, origin):
        target = beside(i)
        return pltpu.make_async_remote_copy(
            src_ref=pair_sum.at[target],
            dst_ref=tile_in.at[origin],
            send_sem=obs2_ss.at[i],
            recv_sem=obs2_rs.at[origin],
            device_id=(p, z, y * GROUP + target),
            device_id_type=MESH,
        )

    def obs3_copy(origin):
        return pltpu.make_async_remote_copy(
            src_ref=tile_in,
            dst_ref=forced_in.at[origin],
            send_sem=obs3_ss.at[0],
            recv_sem=obs3_rs.at[origin],
            device_id=(p, LAYERS - 1, a),
            device_id_type=MESH,
        )

    def send_layers(step, piece):
        @pl.when(has_high)
        def _():
            layer_copy(step, 0, piece).start()

        @pl.when(has_low)
        def _():
            layer_copy(step, 1, piece).start()

    def take_layers(step, piece):
        @pl.when(has_low)
        def _():
            layer_copy(step, 0, piece).wait_recv()

        @pl.when(has_high)
        def _():
            layer_copy(step, 1, piece).wait_recv()

    def send_rows(step, piece):
        @pl.when(has_south)
        def _():
            row_copy(step, 0, piece).start()

        @pl.when(has_north)
        def _():
            row_copy(step, 1, piece).start()

    def take_rows(step, piece):
        @pl.when(has_north)
        def _():
            row_copy(step, 0, piece).wait_recv()

        @pl.when(has_south)
        def _():
            row_copy(step, 1, piece).wait_recv()

    lane_of = iota((ROWS, LANES), 1)
    own_lane = lane_of == lax.rem(a, LANES // ROWS) * ROWS + iota((ROWS, LANES), 0)

    def fill_edges(step):
        for f in range(FIELDS):
            for side in range(2):
                block = scaled[step][f, :, (0 if side == 0 else COLS - LANES):(LANES if side == 0 else COLS)]
                column = block[:, 0:1] if side == 0 else block[:, LANES - 1:LANES]
                wide = jnp.where(own_lane, jnp.broadcast_to(column, (ROWS, LANES)), 0.0)
                edge_out[step, side, f:f + 1, :] = jnp.sum(wide, axis=0, keepdims=True)

    def fill_base(step, source, target):
        rate = [[couple[e, c] for c in range(FIELDS)] for e in range(FIELDS)]
        for b in range(BLOCKS):
            cols = slice(b * LANES, (b + 1) * LANES)
            state = [source[e, :, cols] for e in range(FIELDS)]
            for c in range(FIELDS):
                total = state[c]
                for e in range(FIELDS):
                    total = total + rate[e][c] * state[e]
                target[c, :, cols] = total
        col_of = iota((ROWS, COLS), 1)
        row_of = iota((ROWS, COLS), 0)
        for f in range(FIELDS):
            s = scaled[step][f]
            west = jnp.where(col_of == 0, 0.0, pltpu.roll(s, 1, 1))
            east = jnp.where(col_of == COLS - 1, 0.0, pltpu.roll(s, COLS - 1, 1))
            north = jnp.where(row_of == 0, 0.0, pltpu.roll(s, 1, 0))
            south = jnp.where(row_of == ROWS - 1, 0.0, pltpu.roll(s, ROWS - 1, 0))
            target[f] = target[f] + ((west + east) + (north + south) - 6.0 * s)

    def forward_edges(step):
        for i in range(GROUP):
            edge_copy(step, i, i).wait_recv()
        total = edge_in[step, 0] + edge_in[step, 1] + edge_in[step, 2] + edge_in[step, 3]
        edge_sum[step] = total
        edge_all[step, y] = total
        for i in range(1, LINES):
            line_copy(step, i, y).start()

    def add_ghost(step, target):
        for i in range(1, LINES):
            line_copy(step, i, along_line(i)).wait_recv()
        half = LINES // 2
        for side in range(2):
            for h in range(2):
                total = edge_all[step, h * half, side]
                for i in range(1, half):
                    total = total + edge_all[step, h * half + i, side]
                edge_rows[side, 0:FIELDS, h * LANES:(h + 1) * LANES] = total

        def one_field(f, carry):
            rows = []
            for side in range(2):
                edge = edge_rows[side, pl.ds(f, 1), :]
                for point in range(POINTS):
                    rows.append(edge * ghost_wt[side, point:point + 1, :])
            high, low = spread(high_hot[...], jnp.concatenate(rows, axis=1))
            cells = dot_rows(high, low_hot[...]) + dot_rows(low, low_hot[...])
            for b in range(BLOCKS):
                cols = slice(b * LANES, (b + 1) * LANES)
                target[f, :, cols] = target[f, :, cols] + cells[b * ROWS:(b + 1) * ROWS]
            return carry

        lax.fori_loop(0, FIELDS, one_field, 0)

    for f in range(FIELDS):
        value = (diffus[f] * cond[...]) * adj[f]
        scaled_a[f] = value
        row_out[0, 0, f:f + 1, :] = value[ROWS - 1:ROWS]
        row_out[0, 1, f:f + 1, :] = value[0:1]
    fill_edges(0)

    for step in range(2):
        @pl.when(jnp.logical_not(has_low))
        def _():
            layer_in[step, 0] = jnp.zeros((FIELDS, ROWS, COLS), F32)

        @pl.when(jnp.logical_not(has_high))
        def _():
            layer_in[step, 1] = jnp.zeros((FIELDS, ROWS, COLS), F32)

        @pl.when(jnp.logical_not(has_north))
        def _():
            row_in[step, 0] = jnp.zeros((FIELDS, COLS), F32)

        @pl.when(jnp.logical_not(has_south))
        def _():
            row_in[step, 1] = jnp.zeros((FIELDS, COLS), F32)

    def count(flag):
        return jnp.where(flag, 1, 0)

    expected = (
        GROUP + LINES - 1 + GROUP - 1
        + count(has_low) + count(has_high) + count(has_north) + count(has_south) + count(inner)
    )
    pl.semaphore_wait(barrier, expected)

    for i in range(GROUP):
        edge_copy(0, i, q).start()
    send_rows(0, 0)
    for piece in range(len(PIECES)):
        send_layers(0, piece)

    owner_hot = jnp.where(iota((TILES, OBS), 0) == dest[...], 1.0, 0.0)
    earlier = jnp.where(iota((OBS, OBS), 1) < iota((OBS, OBS), 0), 1.0, 0.0).astype(BF16)
    before = dot_rows(owner_hot.astype(BF16), earlier)
    rank = jnp.sum(owner_hot * before, axis=0, keepdims=True)
    in_slot = rank == iota((SLOTS, OBS), 0, F32)
    number = cell[...]
    in_row = jnp.floor((number.astype(F32) + 0.5) * (1.0 / COLS)).astype(jnp.int32)
    column = number - in_row * COLS
    place = ((lax.shift_right_logical(column, 7) * ROWS + in_row) * LANES + (column & (LANES - 1))).astype(F32)
    payload = []
    for kind in range(3):
        for point in range(POINTS):
            if kind < 2:
                row = misfit[kind:kind + 1, :] * obs_wt[point:point + 1, :]
            else:
                row = place[point:point + 1, :]
            payload.append(jnp.where(in_slot, jnp.broadcast_to(row, (SLOTS, OBS)), 0.0))
    packed = dot_rows(owner_hot, jnp.concatenate(payload, axis=0), lax.Precision.HIGHEST)
    width = SLOTS * POINTS
    own_half = iota((TILES, LANES), 1) // width == lax.rem(y, 2)
    for kind in range(3):
        part = packed[:, kind * width:(kind + 1) * width]
        outbox[:, kind, :] = jnp.where(own_half, jnp.concatenate([part, part], axis=1), 0.0)
    outbox[:, 3, :] = jnp.zeros((TILES, LANES), F32)
    for i in range(1, LINES):
        obs1_copy(i, y).start()
    line_in[y] = outbox[pl.ds(y * GROUP, GROUP)]

    fill_base(0, adj, base)

    for side in range(2):
        for point in range(POINTS):
            at = (side * POINTS + point) * EDGE
            local = ghost_row[side, point:point + 1, :] - a * ROWS
            col = ghost_col[side, point:point + 1, :]
            inside = (local >= 0) & (local < ROWS)
            high = jnp.where(inside, lax.shift_right_logical(col, 7) * ROWS + local, -1)
            low = col & (LANES - 1)
            high_hot[:, at:at + EDGE] = jnp.where(iota((HIGH, EDGE), 0) == high, 1.0, 0.0).astype(BF16)
            low_hot[:, at:at + EDGE] = jnp.where(iota((LANES, EDGE), 0) == low, 1.0, 0.0).astype(BF16)

    forward_edges(0)

    for i in range(1, LINES):
        obs1_copy(i, along_line(i)).wait_recv()
    for i in range(GROUP):
        for pair in range(LINES // 2):
            pair_sum[i, pair] = line_in[2 * pair, i] + line_in[2 * pair + 1, i]
    for i in range(1, GROUP):
        obs2_copy(i, q).start()
    tile_in[q] = pair_sum[q]

    add_ghost(0, base)

    for i in range(1, GROUP):
        obs2_copy(i, beside(i)).wait_recv()

    @pl.when(inner)
    def _():
        obs3_copy(z).start()

    @pl.when(outer)
    def _():
        forced_in[LAYERS - 1] = tile_in[...]
        for i in range(LAYERS - 1):
            obs3_copy(i).wait_recv()
        forcing[...] = jnp.zeros((2, HIGH, LANES), F32)

        def one_layer(layer, carry):
            rows = [[], [], []]
            for i in range(GROUP):
                for pair in range(LINES // 2):
                    for kind in range(3):
                        rows[kind].append(forced_in[layer, i, pair, kind:kind + 1, :])
            first_time, second_time, places = [jnp.concatenate(r, axis=1) for r in rows]
            high = jnp.floor(places * (1.0 / LANES))
            low = places - high * LANES
            size = places.shape[1]
            hot_high = jnp.where(iota((HIGH, size), 0, F32) == high, 1.0, 0.0).astype(BF16)
            hot_low = jnp.where(iota((LANES, size), 0, F32) == low, 1.0, 0.0).astype(BF16)
            for moment, row in enumerate((first_time, second_time)):
                top, rest = spread(hot_high, row)
                forcing[moment] = forcing[moment] + (dot_rows(top, hot_low) + dot_rows(rest, hot_low))
            return carry

        lax.fori_loop(0, LAYERS, one_layer, 0)
        for b in range(BLOCKS):
            cols = slice(b * LANES, (b + 1) * LANES)
            base[FORCED, :, cols] = base[FORCED, :, cols] + forcing[1, b * ROWS:(b + 1) * ROWS]

    def with_halos(value, step, f, cols):
        size = cols.stop - cols.start
        row_of = iota((ROWS, size), 0)
        value = value + (layer_in[step, 0, f, :, cols] + layer_in[step, 1, f, :, cols])
        north = jnp.broadcast_to(row_in[step, 0, f:f + 1, cols], (ROWS, size))
        south = jnp.broadcast_to(row_in[step, 1, f:f + 1, cols], (ROWS, size))
        return value + jnp.where(row_of == 0, north, jnp.where(row_of == ROWS - 1, south, 0.0))

    take_rows(0, 0)
    for g, group in enumerate(GROUPS):
        for piece in group:
            take_layers(0, piece)
            start, stop = PIECES[piece]
            cols = slice(start * LANES, stop * LANES)
            for f in range(FIELDS):
                value = with_halos(base[f, :, cols], 0, f, cols)
                base[f, :, cols] = value
                value = (diffus[f] * cond[:, cols]) * value
                scaled_b[f, :, cols] = value
                row_out[1, 0, f:f + 1, cols] = value[ROWS - 1:ROWS]
                row_out[1, 1, f:f + 1, cols] = value[0:1]
            send_layers(1, piece)
        for piece in ROW_AFTER.get(g, ()):
            send_rows(1, piece)
        if g == 0:
            fill_edges(1)
            for i in range(GROUP):
                edge_copy(1, i, q).start()

    forward_edges(1)
    fill_base(1, base, out)
    add_ghost(1, out)

    @pl.when(outer)
    def _():
        for b in range(BLOCKS):
            cols = slice(b * LANES, (b + 1) * LANES)
            out[FORCED, :, cols] = out[FORCED, :, cols] + forcing[0, b * ROWS:(b + 1) * ROWS]

    for piece in range(len(ROW_PIECES[1])):
        take_rows(1, piece)
    for piece, (start, stop) in enumerate(PIECES):
        take_layers(1, piece)
        cols = slice(start * LANES, stop * LANES)
        for f in range(FIELDS):
            out[f, :, cols] = with_halos(out[f, :, cols], 1, f, cols)

    for step in range(2):
        for i in range(GROUP):
            edge_copy(step, i, q).wait_send()
        for i in range(1, LINES):
            line_copy(step, i, y).wait_send()
    for i in range(1, LINES):
        obs1_copy(i, y).wait_send()
    for i in range(1, GROUP):
        obs2_copy(i, q).wait_send()

    @pl.when(inner)
    def _():
        obs3_copy(z).wait_send()

    for step in range(2):
        for way, flag in ((0, has_high), (1, has_low)):
            @pl.when(flag)
            def _():
                for piece in range(len(PIECES)):
                    layer_copy(step, way, piece).wait_send()

        for way, flag in ((0, has_south), (1, has_north)):
            @pl.when(flag)
            def _():
                for piece in range(len(ROW_PIECES[step])):
                    row_copy(step, way, piece).wait_send()


def steps(*operands):
    vmem = pl.BlockSpec(memory_space=pltpu.VMEM)
    smem = pl.BlockSpec(memory_space=pltpu.SMEM)
    dma = pltpu.SemaphoreType.DMA
    state = (FIELDS, ROWS, COLS)
    terms = 2 * POINTS * EDGE
    pieces, row_pieces = len(PIECES), max(len(r) for r in ROW_PIECES)
    pairs = LINES // 2
    return pl.pallas_call(
        kernel,
        out_shape=jax.ShapeDtypeStruct(state, F32),
        in_specs=[vmem, vmem, smem, smem] + [vmem] * 7,
        out_specs=vmem,
        scratch_shapes=[
            pltpu.VMEM(state, F32),
            pltpu.VMEM(state, F32),
            pltpu.VMEM(state, F32),
            pltpu.VMEM((2, 2) + state, F32),
            pltpu.VMEM((2, 2, FIELDS, COLS), F32),
            pltpu.VMEM((2, 2, FIELDS, COLS), F32),
            pltpu.VMEM((2, 2, FIELDS, LANES), F32),
            pltpu.VMEM((2, GROUP, 2, FIELDS, LANES), F32),
            pltpu.VMEM((2, 2, FIELDS, LANES), F32),
            pltpu.VMEM((2, LINES, 2, FIELDS, LANES), F32),
            pltpu.VMEM((2, 8, EDGE), F32),
            pltpu.VMEM((HIGH, terms), BF16),
            pltpu.VMEM((LANES, terms), BF16),
            pltpu.VMEM((TILES, 4, LANES), F32),
            pltpu.VMEM((LINES, GROUP, 4, LANES), F32),
            pltpu.VMEM((GROUP, pairs, 4, LANES), F32),
            pltpu.VMEM((GROUP, pairs, 4, LANES), F32),
            pltpu.VMEM((LAYERS, GROUP, pairs, 4, LANES), F32),
            pltpu.VMEM((2, HIGH, LANES), F32),
            dma((2, 2, pieces)), dma((2, 2, pieces)),
            dma((2, 2, row_pieces)), dma((2, 2, row_pieces)),
            dma((2, GROUP)), dma((2, GROUP)),
            dma((2, LINES)), dma((2, LINES)),
            dma((LINES,)), dma((LINES,)),
            dma((GROUP,)), dma((GROUP,)),
            dma((1,)), dma((LAYERS,)),
        ],
        compiler_params=pltpu.CompilerParams(
            collective_id=0, has_side_effects=True, vmem_limit_bytes=40 << 20
        ),
        name="adjoint_steps",
    )(*operands)


def body(
    adj_final, cond, diffus, couple, ghost_row, ghost_col, ghost_wt, obs_dest, obs_cell, obs_wt,
    misfit,
):
    final = steps(
        adj_final.reshape(FIELDS, ROWS, COLS), cond[0, 0], diffus, couple, ghost_row, ghost_col,
        ghost_wt, obs_dest.reshape(1, OBS), obs_cell[0, 0], obs_wt[0, 0], misfit[0, 0],
    )
    return final[None, :, None]


def solution(mesh):
    placed = (
        P("panel", None, "rad", "ang", None),
        P("panel", "rad", "ang", None),
        P(),
        P(),
        P(),
        P(),
        P(),
        P("panel", "rad", "ang", None),
        P("panel", "rad", None, "ang"),
        P("panel", "rad", None, "ang"),
        P("panel", "rad", None, "ang"),
    )
    return jax.shard_map(
        body,
        mesh=mesh,
        in_specs=placed,
        out_specs=P("panel", None, "rad", "ang", None),
        check_vma=False,
    )
```

```python
import functools
import jax
import jax.numpy as jnp
from jax import lax
from jax.experimental import pallas as pl
from jax.experimental.pallas import tpu as pltpu
from jax.sharding import PartitionSpec as P

MESH = pl.DeviceIdType.MESH
F32, BF16 = jnp.float32, jnp.bfloat16
FIELDS, ROWS, COLS = 7, 8, 1536
LANES = 128
BLOCKS = COLS // LANES
WIDE = 256
SPANS = COLS // WIDE
HIGH = ROWS * SPANS
LAYERS, TILES, GROUP = 8, 32, 4
LINES = TILES // GROUP
SLOTS = 16
POINTS = 4
OBS = 256
EDGE = TILES * ROWS
FORCED = 3

PIECES = ((0, 512), (512, 1024), (1024, 1536))


def iota(shape, dim, dtype=jnp.int32):
    value = lax.broadcasted_iota(jnp.int32, shape, dim)
    return value if dtype == jnp.int32 else value.astype(dtype)


def dot_rows(a, b, precision=None):
    return lax.dot_general(
        a, b, (((1,), (1,)), ((), ())), precision=precision, preferred_element_type=F32
    )


def indicator(count, row):
    small = row.astype(BF16)
    hot = iota((count, row.shape[1]), 0, F32).astype(BF16) == jnp.broadcast_to(small, (count, row.shape[1]))
    return jnp.where(hot, jnp.ones((), BF16), jnp.zeros((), BF16))


def spread(high_hot, row):
    count, width = high_hot.shape
    wide = jnp.broadcast_to(row, (16, width))
    top = wide.astype(BF16)
    rest = (wide - top.astype(F32)).astype(BF16)
    grid = high_hot.reshape(count // 16, 16, width)
    return [(grid * part[None]).reshape(count, width) for part in (top, rest)]


def kernel(
    adj_hbm, cond_hbm, diffus_hbm, couple_hbm, ghost_row_hbm, ghost_col_hbm, ghost_wt_hbm,
    dest_hbm, cell_hbm, obs_wt_hbm, misfit_hbm,
    out,
    adj, cond, diffus, couple, ghost_row, ghost_col, ghost_wt, dest, cell, obs_wt, misfit, load_s,
    scaled_a, scaled_b, scaled_f, base, layer_in, row_out, row_in,
    edge_out, edge_in, edge_sum, edge_all, edge_rows,
    high_hot, low_hot, spread_rows,
    outbox, line_in, pair_sum, tile_in, forced_in, forcing, late_out, late_in,
    layer_ss, layer_rs, row_ss, row_rs,
    edge_ss, edge_rs, line_ss, line_rs, obs_ss, obs_rs, late_ss, late_rs,
):
    loads = [
        pltpu.make_async_copy(source, target, load_s.at[i])
        for i, (source, target) in enumerate((
            (adj_hbm, adj), (cond_hbm, cond), (diffus_hbm, diffus), (couple_hbm, couple),
            (dest_hbm, dest), (cell_hbm, cell), (obs_wt_hbm, obs_wt), (misfit_hbm, misfit),
            (ghost_row_hbm, ghost_row), (ghost_col_hbm, ghost_col), (ghost_wt_hbm, ghost_wt),
        ))
    ]
    for load in loads[:3]:
        load.start()

    p, z, a = lax.axis_index("panel"), lax.axis_index("rad"), lax.axis_index("ang")
    y, q = a // GROUP, lax.rem(a, GROUP)
    has_low, has_high = z > 0, z < LAYERS - 1
    has_north, has_south = a > 0, a < TILES - 1
    outer = z == LAYERS - 1
    inner = z < LAYERS - 1
    scaled = (scaled_a, scaled_b)

    def along_line(step):
        return lax.rem(y + step, LINES)

    def beside(step):
        return lax.rem(q + step, GROUP)

    barrier = pltpu.get_barrier_semaphore()

    def greet(panel, layer, tile):
        pl.semaphore_signal(barrier, inc=1, device_id=(panel, layer, tile), device_id_type=MESH)

    @pl.when(has_low)
    def _():
        greet(p, z - 1, a)

    @pl.when(has_high)
    def _():
        greet(p, z + 1, a)

    @pl.when(has_north)
    def _():
        greet(p, z, a - 1)

    @pl.when(has_south)
    def _():
        greet(p, z, a + 1)

    for i in range(GROUP):
        greet(1 - p, z, y * GROUP + i)
    for i in range(1, LINES):
        greet(p, z, along_line(i) * GROUP + q)
    for i in range(1, GROUP):
        greet(p, z, y * GROUP + beside(i))

    @pl.when(outer)
    def _():
        for i in range(LAYERS - 1):
            greet(p, i, a)

    for load in loads[3:]:
        load.start()

    def remote(source, target, send, recv, device):
        return pltpu.make_async_remote_copy(
            src_ref=source, dst_ref=target, send_sem=send, recv_sem=recv,
            device_id=device, device_id_type=MESH,
        )

    def layer_copy(step, way, start=0, stop=COLS, piece=0):
        return remote(
            scaled[step].at[:, :, start:stop], layer_in.at[step, way, :, :, start:stop],
            layer_ss.at[step, way], layer_rs.at[step, way, piece],
            (p, z + 1 if way == 0 else z - 1, a),
        )

    def row_copy(step, way):
        return remote(
            row_out.at[step, way], row_in.at[step, way], row_ss.at[step, way], row_rs.at[step, way],
            (p, z, a + 1 if way == 0 else a - 1),
        )

    def edge_copy(step, i):
        return remote(
            edge_out.at[step], edge_in.at[step, q], edge_ss.at[step], edge_rs.at[step],
            (1 - p, z, y * GROUP + i),
        )

    def edges_moved(step):
        everything = edge_in.at[step]
        return remote(everything, everything, edge_ss.at[step], edge_rs.at[step], (1 - p, z, a))

    def line_copy(step, i):
        return remote(
            edge_sum.at[step], edge_all.at[step, y], line_ss.at[step], line_rs.at[step],
            (p, z, along_line(i) * GROUP + q),
        )

    def lines_moved(step):
        others = edge_all.at[step, pl.ds(0, LINES - 1)]
        return remote(others, others, line_ss.at[step], line_rs.at[step], (1 - p, z, a))

    def obs1_copy(i):
        target = along_line(i)
        return remote(
            outbox.at[pl.ds(target * GROUP, GROUP)], line_in.at[y], obs_ss.at[0], obs_rs.at[0],
            (p, z, target * GROUP + q),
        )

    def obs1_moved():
        others = line_in.at[pl.ds(0, LINES - 1)]
        return remote(others, others, obs_ss.at[0], obs_rs.at[0], (1 - p, z, a))

    def obs2_copy(i):
        target = beside(i)
        return remote(
            pair_sum.at[target], tile_in.at[q], obs_ss.at[1], obs_rs.at[1],
            (p, z, y * GROUP + target),
        )

    def obs2_moved():
        others = tile_in.at[pl.ds(0, GROUP - 1)]
        return remote(others, others, obs_ss.at[1], obs_rs.at[1], (1 - p, z, a))

    def obs3_copy():
        return remote(tile_in, forced_in.at[z], obs_ss.at[2], obs_rs.at[2], (p, LAYERS - 1, a))

    def obs3_moved():
        others = forced_in.at[pl.ds(0, LAYERS - 1)]
        return remote(others, others, obs_ss.at[2], obs_rs.at[2], (1 - p, z, a))

    def late_copy():
        return remote(late_out, late_in, late_ss, late_rs, (p, z - 1, a))

    def send_layers(step, piece):
        start, stop = PIECES[piece]

        @pl.when(has_high)
        def _():
            layer_copy(step, 0, start, stop, piece).start()

        @pl.when(has_low)
        def _():
            layer_copy(step, 1, start, stop, piece).start()

    def take_layers(step, piece):
        start, stop = PIECES[piece]

        @pl.when(has_low)
        def _():
            layer_copy(step, 0, start, stop, piece).wait_recv()

        @pl.when(has_high)
        def _():
            layer_copy(step, 1, start, stop, piece).wait_recv()

    def send_rows(step):
        @pl.when(has_south)
        def _():
            row_copy(step, 0).start()

        @pl.when(has_north)
        def _():
            row_copy(step, 1).start()

    def take_rows(step):
        @pl.when(has_north)
        def _():
            row_copy(step, 0).wait_recv()

        @pl.when(has_south)
        def _():
            row_copy(step, 1).wait_recv()

    own_lane = iota((ROWS, LANES), 1) == (
        lax.rem(a, LANES // ROWS) * ROWS + iota((ROWS, LANES), 0)
    )

    def field_of(step, f):
        return scaled_f if step == 1 and f == FORCED else scaled[step].at[f]

    def fill_rows(step):
        for f in range(FIELDS):
            row_out[step, 0, f:f + 1, :] = field_of(step, f)[ROWS - 1:ROWS, :]
            row_out[step, 1, f:f + 1, :] = field_of(step, f)[0:1, :]

    def fill_edges(step):
        for f in range(FIELDS):
            for side, at in ((0, 0), (1, COLS - 1)):
                start = at // LANES * LANES
                block = field_of(step, f)[:, start:start + LANES]
                column = block[:, at - start:at - start + 1]
                wide = jnp.where(own_lane, jnp.broadcast_to(column, (ROWS, LANES)), 0.0)
                edge_out[step, side, f:f + 1, :] = jnp.sum(wide, axis=0, keepdims=True)

    def fill_base(step, source, target):
        rate = [[couple[e, c] for c in range(FIELDS)] for e in range(FIELDS)]
        for b in range(BLOCKS):
            cols = slice(b * LANES, (b + 1) * LANES)
            state = [source[e, :, cols] for e in range(FIELDS)]
            for c in range(FIELDS):
                total = state[c]
                for e in range(FIELDS):
                    total = total + rate[e][c] * state[e]
                target[c, :, cols] = total
        col_of = iota((ROWS, COLS), 1)
        row_of = iota((ROWS, COLS), 0)
        for f in range(FIELDS):
            s = field_of(step, f)[...]
            west = jnp.where(col_of == 0, 0.0, pltpu.roll(s, 1, 1))
            east = jnp.where(col_of == COLS - 1, 0.0, pltpu.roll(s, COLS - 1, 1))
            north = jnp.where(row_of == 0, 0.0, pltpu.roll(s, 1, 0))
            south = jnp.where(row_of == ROWS - 1, 0.0, pltpu.roll(s, ROWS - 1, 0))
            target[f] = target[f] + ((west + east) + (north + south) - 6.0 * s)

    def forward_edges(step):
        edges_moved(step).wait_recv()
        total = edge_in[step, 0] + edge_in[step, 1] + edge_in[step, 2] + edge_in[step, 3]
        edge_sum[step] = total
        for i in range(1, LINES):
            line_copy(step, i).start()
        edge_all[step, y] = total

    def add_ghost(step, target):
        lines_moved(step).wait_recv()
        half = LINES // 2
        for side in range(2):
            for h in range(2):
                total = edge_all[step, h * half, side]
                for i in range(1, half):
                    total = total + edge_all[step, h * half + i, side]
                edge_rows[side, 0:FIELDS, h * LANES:(h + 1) * LANES] = total
        for f in range(FIELDS):
            rows = [
                edge_rows[side, f:f + 1, :] * ghost_wt[side, point:point + 1, :]
                for side in range(2) for point in range(POINTS)
            ]
            top, rest = spread(high_hot[...], jnp.concatenate(rows, axis=1))
            spread_rows[f * HIGH:(f + 1) * HIGH] = top
            spread_rows[(FIELDS + f) * HIGH:(FIELDS + f + 1) * HIGH] = rest
        cells = dot_rows(spread_rows[...], low_hot[...])
        for f in range(FIELDS):
            for b in range(SPANS):
                at = f * HIGH + b * ROWS
                more = at + FIELDS * HIGH
                cols = slice(b * WIDE, (b + 1) * WIDE)
                target[f, :, cols] = target[f, :, cols] + (
                    cells[at:at + ROWS] + cells[more:more + ROWS]
                )

    for load in loads[:3]:
        load.wait()
    for f in range(FIELDS):
        scaled_a[f] = (diffus[f] * cond[...]) * adj[f]

    def count(flag):
        return jnp.where(flag, 1, 0)

    expected = (
        GROUP + LINES - 1 + GROUP - 1
        + count(has_low) + count(has_high) + count(has_north) + count(has_south) + count(inner)
    )
    pl.semaphore_wait(barrier, expected)

    for piece in range(len(PIECES)):
        send_layers(0, piece)
    fill_edges(0)
    for i in range(GROUP):
        edge_copy(0, i).start()
    fill_rows(0)
    send_rows(0)

    for load in loads[3:]:
        load.wait()
    owner_hot = jnp.where(iota((TILES, OBS), 0) == dest[...], 1.0, 0.0)
    earlier = jnp.where(iota((OBS, OBS), 1) < iota((OBS, OBS), 0), 1.0, 0.0).astype(BF16)
    before = dot_rows(owner_hot.astype(BF16), earlier)
    rank = jnp.sum(owner_hot * before, axis=0, keepdims=True)
    in_slot = rank == iota((SLOTS, OBS), 0, F32)
    number = cell[...]
    in_row = jnp.floor((number.astype(F32) + 0.5) * (1.0 / COLS)).astype(jnp.int32)
    column = number - in_row * COLS
    place = (
        (lax.shift_right_logical(column, 8) * ROWS + in_row) * WIDE + (column & (WIDE - 1))
    ).astype(F32)
    payload = []
    for kind in range(3):
        for point in range(POINTS):
            if kind < 2:
                row = misfit[kind:kind + 1, :] * obs_wt[point:point + 1, :]
            else:
                row = place[point:point + 1, :]
            payload.append(jnp.where(in_slot, jnp.broadcast_to(row, (SLOTS, OBS)), 0.0))
    packed = dot_rows(owner_hot, jnp.concatenate(payload, axis=0), lax.Precision.HIGHEST)
    width = SLOTS * POINTS
    own_half = iota((TILES, LANES), 1) // width == lax.rem(y, 2)
    for kind in range(3):
        part = packed[:, kind * width:(kind + 1) * width]
        outbox[:, kind, :] = jnp.where(own_half, jnp.concatenate([part, part], axis=1), 0.0)
    outbox[:, 3, :] = jnp.zeros((TILES, LANES), F32)
    for i in range(1, LINES):
        obs1_copy(i).start()
    line_in[y] = outbox[pl.ds(y * GROUP, GROUP)]

    forward_edges(0)

    for step in range(2):
        @pl.when(jnp.logical_not(has_low))
        def _():
            layer_in[step, 0] = jnp.zeros((FIELDS, ROWS, COLS), F32)

        @pl.when(jnp.logical_not(has_high))
        def _():
            layer_in[step, 1] = jnp.zeros((FIELDS, ROWS, COLS), F32)

        @pl.when(jnp.logical_not(has_north))
        def _():
            row_in[step, 0] = jnp.zeros((FIELDS, COLS), F32)

        @pl.when(jnp.logical_not(has_south))
        def _():
            row_in[step, 1] = jnp.zeros((FIELDS, COLS), F32)

    for side in range(2):
        for point in range(POINTS):
            at = (side * POINTS + point) * EDGE
            local = ghost_row[side, point:point + 1, :] - a * ROWS
            col = ghost_col[side, point:point + 1, :]
            inside = (local >= 0) & (local < ROWS)
            high = jnp.where(inside, lax.shift_right_logical(col, 8) * ROWS + local, -1)
            low = col & (WIDE - 1)
            high_hot[:, at:at + EDGE] = indicator(HIGH, high.astype(F32))
            low_hot[:, at:at + EDGE] = indicator(WIDE, low.astype(F32))

    obs1_moved().wait_recv()
    for i in range(GROUP):
        for pair in range(LINES // 2):
            pair_sum[i, pair] = line_in[2 * pair, i] + line_in[2 * pair + 1, i]
    for i in range(1, GROUP):
        obs2_copy(i).start()
    tile_in[q] = pair_sum[q]

    fill_base(0, adj, base)
    add_ghost(0, base)

    obs2_moved().wait_recv()

    @pl.when(inner)
    def _():
        obs3_copy().start()

    def with_halos(value, step, f, start, stop):
        size = stop - start
        row_of = iota((ROWS, size), 0)
        value = value + (layer_in[step, 0, f, :, start:stop] + layer_in[step, 1, f, :, start:stop])
        north = jnp.broadcast_to(row_in[step, 0, f:f + 1, start:stop], (ROWS, size))
        south = jnp.broadcast_to(row_in[step, 1, f:f + 1, start:stop], (ROWS, size))
        return value + jnp.where(row_of == 0, north, jnp.where(row_of == ROWS - 1, south, 0.0))

    take_rows(0)
    for piece, (start, stop) in enumerate(PIECES):
        take_layers(0, piece)
        for f in range(FIELDS):
            value = with_halos(base[f, :, start:stop], 0, f, start, stop)
            base[f, :, start:stop] = value
            scaled_b[f, :, start:stop] = (diffus[f] * cond[:, start:stop]) * value
        send_layers(1, piece)
    scaled_f[...] = scaled_b[FORCED]

    @pl.when(outer)
    def _():
        forced_in[LAYERS - 1] = tile_in[...]
        obs3_moved().wait_recv()
        forcing[...] = jnp.zeros((2 * HIGH, WIDE), F32)

        def one_layer(layer, carry):
            rows = [[], [], []]
            for i in range(GROUP):
                for pair in range(LINES // 2):
                    for kind in range(3):
                        rows[kind].append(forced_in[layer, i, pair, kind:kind + 1, :])
            early, late, places = [jnp.concatenate(r, axis=1) for r in rows]
            high = jnp.floor(places * (1.0 / WIDE))
            hot_high = indicator(HIGH, high)
            hot_low = indicator(WIDE, places - high * WIDE)
            top_a, rest_a = spread(hot_high, early)
            top_b, rest_b = spread(hot_high, late)
            cells = dot_rows(jnp.concatenate([top_a, top_b, rest_a, rest_b], axis=0), hot_low)
            forcing[...] = forcing[...] + (cells[:2 * HIGH] + cells[2 * HIGH:])
            return carry

        lax.fori_loop(0, LAYERS, one_layer, 0, unroll=2)
        for b in range(SPANS):
            cols = slice(b * WIDE, (b + 1) * WIDE)
            added = forcing[HIGH + b * ROWS:HIGH + (b + 1) * ROWS]
            share = (diffus[FORCED] * cond[:, cols]) * added
            base[FORCED, :, cols] = base[FORCED, :, cols] + added
            scaled_f[:, cols] = scaled_f[:, cols] + share
            late_out[:, cols] = share
        late_copy().start()

    fill_edges(1)
    for i in range(GROUP):
        edge_copy(1, i).start()
    fill_rows(1)
    send_rows(1)
    fill_base(1, base, out)
    forward_edges(1)
    add_ghost(1, out)

    @pl.when(outer)
    def _():
        for b in range(SPANS):
            cols = slice(b * WIDE, (b + 1) * WIDE)
            out[FORCED, :, cols] = out[FORCED, :, cols] + forcing[b * ROWS:(b + 1) * ROWS]

    take_rows(1)
    for piece, (start, stop) in enumerate(PIECES):
        take_layers(1, piece)
        for f in range(FIELDS):
            out[f, :, start:stop] = with_halos(out[f, :, start:stop], 1, f, start, stop)

    @pl.when(z == LAYERS - 2)
    def _():
        late_copy().wait_recv()
        out[FORCED] = out[FORCED] + late_in[...]

    for step in range(2):
        edges_moved(step).wait_send()
        lines_moved(step).wait_send()
        for way, flag in ((0, has_high), (1, has_low)):
            @pl.when(flag)
            def _():
                layer_copy(step, way).wait_send()

        for way, flag in ((0, has_south), (1, has_north)):
            @pl.when(flag)
            def _():
                row_copy(step, way).wait_send()

    obs1_moved().wait_send()
    obs2_moved().wait_send()

    @pl.when(inner)
    def _():
        obs3_copy().wait_send()

    @pl.when(outer)
    def _():
        late_copy().wait_send()


def steps(*operands):
    dma = pltpu.SemaphoreType.DMA
    state = (FIELDS, ROWS, COLS)
    terms = 2 * POINTS * EDGE
    pairs = LINES // 2
    inputs = [
        pltpu.SMEM(x.shape, x.dtype) if i in (2, 3) else pltpu.VMEM(x.shape, x.dtype)
        for i, x in enumerate(operands)
    ]
    return pl.pallas_call(
        kernel,
        out_shape=jax.ShapeDtypeStruct(state, F32),
        in_specs=[pl.BlockSpec(memory_space=pltpu.HBM)] * len(operands),
        out_specs=pl.BlockSpec(memory_space=pltpu.VMEM),
        scratch_shapes=inputs + [
            dma((len(operands),)),
            pltpu.VMEM(state, F32),
            pltpu.VMEM(state, F32),
            pltpu.VMEM(state[1:], F32),
            pltpu.VMEM(state, F32),
            pltpu.VMEM((2, 2) + state, F32),
            pltpu.VMEM((2, 2, FIELDS, COLS), F32),
            pltpu.VMEM((2, 2, FIELDS, COLS), F32),
            pltpu.VMEM((2, 2, FIELDS, LANES), F32),
            pltpu.VMEM((2, GROUP, 2, FIELDS, LANES), F32),
            pltpu.VMEM((2, 2, FIELDS, LANES), F32),
            pltpu.VMEM((2, LINES, 2, FIELDS, LANES), F32),
            pltpu.VMEM((2, 8, EDGE), F32),
            pltpu.VMEM((HIGH, terms), BF16),
            pltpu.VMEM((WIDE, terms), BF16),
            pltpu.VMEM((2 * FIELDS * HIGH, terms), BF16),
            pltpu.VMEM((TILES, 4, LANES), F32),
            pltpu.VMEM((LINES, GROUP, 4, LANES), F32),
            pltpu.VMEM((GROUP, pairs, 4, LANES), F32),
            pltpu.VMEM((GROUP, pairs, 4, LANES), F32),
            pltpu.VMEM((LAYERS, GROUP, pairs, 4, LANES), F32),
            pltpu.VMEM((2 * HIGH, WIDE), F32),
            pltpu.VMEM(state[1:], F32),
            pltpu.VMEM(state[1:], F32),
            dma((2, 2)), dma((2, 2, len(PIECES))),
            dma((2, 2)), dma((2, 2)),
            dma((2,)), dma((2,)),
            dma((2,)), dma((2,)),
            dma((3,)), dma((3,)),
            dma(()), dma(()),
        ],
        compiler_params=pltpu.CompilerParams(
            collective_id=0, has_side_effects=True, vmem_limit_bytes=60 << 20
        ),
        name="adjoint_steps",
    )(*operands)


def body(
    adj_final, cond, diffus, couple, ghost_row, ghost_col, ghost_wt, obs_dest, obs_cell, obs_wt,
    misfit,
):
    final = steps(
        adj_final.reshape(FIELDS, ROWS, COLS), cond[0, 0], diffus, couple, ghost_row, ghost_col,
        ghost_wt, obs_dest.reshape(1, OBS), obs_cell[0, 0], obs_wt[0, 0], misfit[0, 0],
    )
    return final[None, :, None]


def solution(mesh):
    placed = (
        P("panel", None, "rad", "ang", None),
        P("panel", "rad", "ang", None),
        P(),
        P(),
        P(),
        P(),
        P(),
        P("panel", "rad", "ang", None),
        P("panel", "rad", None, "ang"),
        P("panel", "rad", None, "ang"),
        P("panel", "rad", None, "ang"),
    )
    return jax.shard_map(
        body,
        mesh=mesh,
        in_specs=placed,
        out_specs=P("panel", None, "rad", "ang", None),
        check_vma=False,
    )
```

```python
import functools
import jax
import jax.numpy as jnp
from jax import lax
from jax.experimental import pallas as pl
from jax.experimental.pallas import tpu as pltpu
from jax.sharding import PartitionSpec as P

MESH = pl.DeviceIdType.MESH
F32, BF16 = jnp.float32, jnp.bfloat16
FIELDS, ROWS, COLS = 7, 8, 1536
LANES = 128
BLOCKS = COLS // LANES
WIDE = 256
SPANS = COLS // WIDE
HIGH = ROWS * SPANS
LAYERS, TILES, GROUP = 8, 32, 4
LINES = TILES // GROUP
HALF = LAYERS // 2
SLOTS = 16
POINTS = 4
OBS = 256
EDGE = TILES * ROWS
FORCED = 3

PIECES = ((0, 128), (1408, 1536), (128, 1408))
EDGE_PIECES = 2


def iota(shape, dim, dtype=jnp.int32):
    value = lax.broadcasted_iota(jnp.int32, shape, dim)
    return value if dtype == jnp.int32 else value.astype(dtype)


def dot_rows(a, b, precision=None):
    return lax.dot_general(
        a, b, (((1,), (1,)), ((), ())), precision=precision, preferred_element_type=F32
    )


def indicator(count, row):
    small = row.astype(BF16)
    hot = iota((count, row.shape[1]), 0, F32).astype(BF16) == jnp.broadcast_to(small, (count, row.shape[1]))
    return jnp.where(hot, jnp.ones((), BF16), jnp.zeros((), BF16))


def spread(high_hot, row):
    count, width = high_hot.shape
    wide = jnp.broadcast_to(row, (16, width))
    top = wide.astype(BF16)
    rest = (wide - top.astype(F32)).astype(BF16)
    grid = high_hot.reshape(count // 16, 16, width)
    return [(grid * part[None]).reshape(count, width) for part in (top, rest)]


def kernel(
    adj_hbm, cond_hbm, diffus_hbm, couple_hbm, ghost_row_hbm, ghost_col_hbm, ghost_wt_hbm,
    dest_hbm, cell_hbm, obs_wt_hbm, misfit_hbm,
    out,
    adj, cond, diffus, couple, ghost_row, ghost_col, ghost_wt, dest, cell, obs_wt, misfit, load_s,
    scaled_a, scaled_b, scaled_f, base, layer_in, row_out, row_in,
    edge_out, edge_all, edge_rows,
    high_hot, low_hot, spread_rows,
    outbox, line_in, pair_sum, tile_in, forced_in, forcing, late_out, late_in,
    layer_ss, layer_rs, row_ss, row_rs,
    edge_ss, edge_rs, obs_ss, obs_rs, late_ss, late_rs, open_s,
):
    loads = [
        pltpu.make_async_copy(source, target, load_s.at[i])
        for i, (source, target) in enumerate((
            (adj_hbm, adj), (cond_hbm, cond), (diffus_hbm, diffus), (couple_hbm, couple),
            (dest_hbm, dest), (cell_hbm, cell), (obs_wt_hbm, obs_wt), (misfit_hbm, misfit),
            (ghost_row_hbm, ghost_row), (ghost_col_hbm, ghost_col), (ghost_wt_hbm, ghost_wt),
        ))
    ]
    for load in loads[:3]:
        load.start()

    p, z, a = lax.axis_index("panel"), lax.axis_index("rad"), lax.axis_index("ang")
    y, q = a // GROUP, lax.rem(a, GROUP)
    has_low, has_high = z > 0, z < LAYERS - 1
    has_north, has_south = a > 0, a < TILES - 1
    outer = z == LAYERS - 1
    inner = z < LAYERS - 1
    scaled = (scaled_a, scaled_b)

    def along_line(step):
        return lax.rem(y + step, LINES)

    def beside(step):
        return lax.rem(q + step, GROUP)

    barrier = pltpu.get_barrier_semaphore()

    def greet(panel, layer, tile):
        pl.semaphore_signal(barrier, inc=1, device_id=(panel, layer, tile), device_id_type=MESH)

    order = sorted(range(TILES), key=lambda i: -min(i, TILES - i))
    for i in order:
        greet(1 - p, z, lax.rem(a + i, TILES))
    for i in sorted(range(1, LINES), key=lambda i: -min(i, LINES - i)):
        greet(p, z, along_line(i) * GROUP + q)

    @pl.when(has_low)
    def _():
        greet(p, z - 1, a)

    @pl.when(has_high)
    def _():
        greet(p, z + 1, a)

    @pl.when(has_north)
    def _():
        greet(p, z, a - 1)

    @pl.when(has_south)
    def _():
        greet(p, z, a + 1)

    for i in range(1, GROUP):
        greet(p, z, y * GROUP + beside(i))

    @pl.when(inner)
    def _():
        greet(p, LAYERS - 1, a)

    for load in loads[3:]:
        load.start()

    def remote(source, target, send, recv, device):
        return pltpu.make_async_remote_copy(
            src_ref=source, dst_ref=target, send_sem=send, recv_sem=recv,
            device_id=device, device_id_type=MESH,
        )

    def layer_copy(step, way, start=0, stop=COLS, piece=0):
        return remote(
            scaled[step].at[:, :, start:stop], layer_in.at[step, way, :, :, start:stop],
            layer_ss.at[step, way], layer_rs.at[step, way, piece],
            (p, z + 1 if way == 0 else z - 1, a),
        )

    def row_copy(step, way):
        return remote(
            row_out.at[step, way], row_in.at[step, way], row_ss.at[step, way], row_rs.at[step, way],
            (p, z, a + 1 if way == 0 else a - 1),
        )

    def edge_copy(step, i):
        return remote(
            edge_out.at[step], edge_all.at[step, pl.ds(a, 1), :], edge_ss.at[step], edge_rs.at[step],
            (1 - p, z, lax.rem(a + i, TILES)),
        )

    def edges_moved(step):
        everything = edge_all.at[step]
        return remote(everything, everything, edge_ss.at[step], edge_rs.at[step], (1 - p, z, a))

    def obs1_copy(i):
        target = along_line(i)
        return remote(
            outbox.at[pl.ds(target * GROUP, GROUP)], line_in.at[y], obs_ss.at[0], obs_rs.at[0],
            (p, z, target * GROUP + q),
        )

    def obs1_moved():
        others = line_in.at[pl.ds(0, LINES - 1)]
        return remote(others, others, obs_ss.at[0], obs_rs.at[0], (1 - p, z, a))

    def obs2_copy(i):
        target = beside(i)
        return remote(
            pair_sum.at[target], tile_in.at[q], obs_ss.at[1], obs_rs.at[1],
            (p, z, y * GROUP + target),
        )

    def obs2_moved():
        others = tile_in.at[pl.ds(0, GROUP - 1)]
        return remote(others, others, obs_ss.at[1], obs_rs.at[1], (1 - p, z, a))

    def obs3_copy():
        return remote(
            tile_in, forced_in.at[z], obs_ss.at[2], obs_rs.at[2 + z // HALF], (p, LAYERS - 1, a)
        )

    def obs3_moved(start, count):
        others = forced_in.at[pl.ds(start, count)]
        return remote(
            others, others, obs_ss.at[2], obs_rs.at[2 + start // HALF], (1 - p, z, a)
        )

    def late_copy():
        return remote(late_out, late_in, late_ss, late_rs, (p, z - 1, a))

    def send_layers(step, piece):
        start, stop = PIECES[piece]

        @pl.when(has_high)
        def _():
            layer_copy(step, 0, start, stop, piece).start()

        @pl.when(has_low)
        def _():
            layer_copy(step, 1, start, stop, piece).start()

    def take_layers(step, piece):
        start, stop = PIECES[piece]

        @pl.when(has_low)
        def _():
            layer_copy(step, 0, start, stop, piece).wait_recv()

        @pl.when(has_high)
        def _():
            layer_copy(step, 1, start, stop, piece).wait_recv()

    def send_rows(step):
        @pl.when(has_south)
        def _():
            row_copy(step, 0).start()

        @pl.when(has_north)
        def _():
            row_copy(step, 1).start()

    def take_rows(step):
        @pl.when(has_north)
        def _():
            row_copy(step, 0).wait_recv()

        @pl.when(has_south)
        def _():
            row_copy(step, 1).wait_recv()

    def field_of(step, f):
        return scaled_f if step == 1 and f == FORCED else scaled[step].at[f]

    runs = LANES // ROWS
    lane_of = iota((ROWS, LANES), 1)
    own_run = jnp.where(
        lax.rem(lane_of, ROWS) == iota((ROWS, LANES), 0),
        lax.rem(lane_of // ROWS - lax.rem(a, runs) + runs, runs), -1,
    )
    sent_run = lax.rem(iota((runs, LANES), 1) // ROWS - iota((runs, LANES), 0) + runs, runs)

    def fill_rows(step):
        for f in range(FIELDS):
            row_out[step, 0, f:f + 1, :] = field_of(step, f)[ROWS - 1:ROWS, :]
            row_out[step, 1, f:f + 1, :] = field_of(step, f)[0:1, :]

    def fill_edges(step):
        wide = jnp.zeros((ROWS, LANES), F32)
        for f in range(FIELDS):
            for side, at in ((0, 0), (1, COLS - 1)):
                start = at // LANES * LANES
                block = field_of(step, f)[:, start:start + LANES]
                column = block[:, at - start:at - start + 1]
                wide = jnp.where(
                    own_run == 2 * f + side, jnp.broadcast_to(column, (ROWS, LANES)), wide
                )
        edge_out[step] = jnp.sum(wide, axis=0, keepdims=True)

    def send_edges(step):
        fill_edges(step)
        for i in order:
            edge_copy(step, i).start()

    def fill_base(step, source, target):
        rate = [[couple[e, c] for c in range(FIELDS)] for e in range(FIELDS)]
        for b in range(BLOCKS):
            cols = slice(b * LANES, (b + 1) * LANES)
            state = [source[e, :, cols] for e in range(FIELDS)]
            for c in range(FIELDS):
                total = state[c]
                for e in range(FIELDS):
                    total = total + rate[e][c] * state[e]
                target[c, :, cols] = total
        col_of = iota((ROWS, COLS), 1)
        row_of = iota((ROWS, COLS), 0)
        for f in range(FIELDS):
            s = field_of(step, f)[...]
            west = jnp.where(col_of == 0, 0.0, pltpu.roll(s, 1, 1))
            east = jnp.where(col_of == COLS - 1, 0.0, pltpu.roll(s, COLS - 1, 1))
            north = jnp.where(row_of == 0, 0.0, pltpu.roll(s, 1, 0))
            south = jnp.where(row_of == ROWS - 1, 0.0, pltpu.roll(s, ROWS - 1, 0))
            target[f] = target[f] + ((west + east) + (north + south) - 6.0 * s)

    def add_ghost(step, target):
        edges_moved(step).wait_recv()
        for f in range(FIELDS):
            for side in range(2):
                run = 2 * f + side
                for h in range(2):
                    part = jnp.where(
                        sent_run == run, edge_all[step, h * runs:(h + 1) * runs, :], 0.0
                    )
                    line = jnp.sum(part, axis=0, keepdims=True)
                    if run:
                        line = pltpu.roll(line, LANES - ROWS * run, 1)
                    edge_rows[side, f:f + 1, h * LANES:(h + 1) * LANES] = line
        for f in range(FIELDS):
            rows = [
                edge_rows[side, f:f + 1, :] * ghost_wt[side, point:point + 1, :]
                for side in range(2) for point in range(POINTS)
            ]
            top, rest = spread(high_hot[...], jnp.concatenate(rows, axis=1))
            spread_rows[f * HIGH:(f + 1) * HIGH] = top
            spread_rows[(FIELDS + f) * HIGH:(FIELDS + f + 1) * HIGH] = rest
        cells = dot_rows(spread_rows[...], low_hot[...])
        for f in range(FIELDS):
            for b in range(SPANS):
                at = f * HIGH + b * ROWS
                more = at + FIELDS * HIGH
                cols = slice(b * WIDE, (b + 1) * WIDE)
                target[f, :, cols] = target[f, :, cols] + (
                    cells[at:at + ROWS] + cells[more:more + ROWS]
                )

    for load in loads[:3]:
        load.wait()
    for f in range(FIELDS):
        scaled_a[f] = (diffus[f] * cond[...]) * adj[f]

    fill_edges(0)
    fill_rows(0)

    for load in loads[3:]:
        load.wait()
    owner_hot = jnp.where(iota((TILES, OBS), 0) == dest[...], 1.0, 0.0)
    earlier = jnp.where(iota((OBS, OBS), 1) < iota((OBS, OBS), 0), 1.0, 0.0).astype(BF16)
    before = dot_rows(owner_hot.astype(BF16), earlier)
    rank = jnp.sum(owner_hot * before, axis=0, keepdims=True)
    in_slot = rank == iota((SLOTS, OBS), 0, F32)
    number = cell[...]
    in_row = jnp.floor((number.astype(F32) + 0.5) * (1.0 / COLS)).astype(jnp.int32)
    column = number - in_row * COLS
    place = (
        (lax.shift_right_logical(column, 8) * ROWS + in_row) * WIDE + (column & (WIDE - 1))
    ).astype(F32)
    payload = []
    for kind in range(3):
        for point in range(POINTS):
            if kind < 2:
                row = misfit[kind:kind + 1, :] * obs_wt[point:point + 1, :]
            else:
                row = place[point:point + 1, :]
            payload.append(jnp.where(in_slot, jnp.broadcast_to(row, (SLOTS, OBS)), 0.0))
    packed = dot_rows(owner_hot, jnp.concatenate(payload, axis=0), lax.Precision.HIGHEST)
    width = SLOTS * POINTS
    own_half = iota((TILES, LANES), 1) // width == lax.rem(y, 2)
    for kind in range(3):
        part = packed[:, kind * width:(kind + 1) * width]
        outbox[:, kind, :] = jnp.where(own_half, jnp.concatenate([part, part], axis=1), 0.0)
    outbox[:, 3, :] = jnp.zeros((TILES, LANES), F32)
    for side in range(2):
        for point in range(POINTS):
            at = (side * POINTS + point) * EDGE
            local = ghost_row[side, point:point + 1, :] - a * ROWS
            col = ghost_col[side, point:point + 1, :]
            inside = (local >= 0) & (local < ROWS)
            high = jnp.where(inside, lax.shift_right_logical(col, 8) * ROWS + local, -1)
            low = col & (WIDE - 1)
            high_hot[:, at:at + EDGE] = indicator(HIGH, high.astype(F32))
            low_hot[:, at:at + EDGE] = indicator(WIDE, low.astype(F32))

    def count(flag):
        return jnp.where(flag, 1, 0)

    expected = (
        TILES + LINES - 1 + GROUP - 1
        + count(has_low) + count(has_high) + count(has_north) + count(has_south)
        + jnp.where(outer, LAYERS - 1, 0)
    )
    pl.semaphore_wait(barrier, expected)

    @pl.when(outer)
    def _():
        for i in range(LAYERS - 1):
            pl.semaphore_signal(open_s, inc=1, device_id=(p, i, a), device_id_type=MESH)

    for i in range(1, LINES):
        obs1_copy(i).start()
    line_in[y] = outbox[pl.ds(y * GROUP, GROUP)]

    for i in order:
        edge_copy(0, i).start()
    for piece in range(EDGE_PIECES + 1):
        send_layers(0, piece)
    send_rows(0)

    obs1_moved().wait_recv()
    for i in range(GROUP):
        for pair in range(LINES // 2):
            pair_sum[i, pair] = line_in[2 * pair, i] + line_in[2 * pair + 1, i]
    for i in range(1, GROUP):
        obs2_copy(i).start()
    tile_in[q] = pair_sum[q]

    for step in range(2):
        @pl.when(jnp.logical_not(has_low))
        def _():
            layer_in[step, 0] = jnp.zeros((FIELDS, ROWS, COLS), F32)

        @pl.when(jnp.logical_not(has_high))
        def _():
            layer_in[step, 1] = jnp.zeros((FIELDS, ROWS, COLS), F32)

        @pl.when(jnp.logical_not(has_north))
        def _():
            row_in[step, 0] = jnp.zeros((FIELDS, COLS), F32)

        @pl.when(jnp.logical_not(has_south))
        def _():
            row_in[step, 1] = jnp.zeros((FIELDS, COLS), F32)

    fill_base(0, adj, base)
    obs2_moved().wait_recv()

    @pl.when(inner)
    def _():
        pl.semaphore_wait(open_s, 1)
        obs3_copy().start()

    add_ghost(0, base)

    def one_layer(layer, carry):
        rows = [[], [], []]
        for i in range(GROUP):
            for pair in range(LINES // 2):
                for kind in range(3):
                    rows[kind].append(forced_in[layer, i, pair, kind:kind + 1, :])
        early, late, places = [jnp.concatenate(r, axis=1) for r in rows]
        high = jnp.floor(places * (1.0 / WIDE))
        hot_high = indicator(HIGH, high)
        hot_low = indicator(WIDE, places - high * WIDE)
        top_a, rest_a = spread(hot_high, early)
        top_b, rest_b = spread(hot_high, late)
        cells = dot_rows(jnp.concatenate([top_a, top_b, rest_a, rest_b], axis=0), hot_low)
        forcing[...] = forcing[...] + (cells[:2 * HIGH] + cells[2 * HIGH:])
        return carry

    @pl.when(outer)
    def _():
        forcing[...] = jnp.zeros((2 * HIGH, WIDE), F32)
        obs3_moved(0, HALF).wait_recv()
        lax.fori_loop(0, HALF, one_layer, 0, unroll=2)

    def with_halos(value, step, f, start, stop):
        size = stop - start
        row_of = iota((ROWS, size), 0)
        value = value + (layer_in[step, 0, f, :, start:stop] + layer_in[step, 1, f, :, start:stop])
        north = jnp.broadcast_to(row_in[step, 0, f:f + 1, start:stop], (ROWS, size))
        south = jnp.broadcast_to(row_in[step, 1, f:f + 1, start:stop], (ROWS, size))
        return value + jnp.where(row_of == 0, north, jnp.where(row_of == ROWS - 1, south, 0.0))

    take_rows(0)
    for piece, (start, stop) in enumerate(PIECES):
        take_layers(0, piece)
        for f in range(FIELDS):
            value = with_halos(base[f, :, start:stop], 0, f, start, stop)
            base[f, :, start:stop] = value
            scaled_b[f, :, start:stop] = (diffus[f] * cond[:, start:stop]) * value
        send_layers(1, piece)
        if piece == EDGE_PIECES - 1:
            scaled_f[:, :LANES] = scaled_b[FORCED, :, :LANES]
            scaled_f[:, COLS - LANES:] = scaled_b[FORCED, :, COLS - LANES:]

            @pl.when(inner)
            def _():
                send_edges(1)
    scaled_f[...] = scaled_b[FORCED]

    @pl.when(outer)
    def _():
        forced_in[LAYERS - 1] = tile_in[...]
        obs3_moved(HALF, HALF - 1).wait_recv()
        lax.fori_loop(HALF, LAYERS, one_layer, 0, unroll=2)
        for b in range(SPANS):
            cols = slice(b * WIDE, (b + 1) * WIDE)
            added = forcing[HIGH + b * ROWS:HIGH + (b + 1) * ROWS]
            share = (diffus[FORCED] * cond[:, cols]) * added
            base[FORCED, :, cols] = base[FORCED, :, cols] + added
            scaled_f[:, cols] = scaled_f[:, cols] + share
            late_out[:, cols] = share
        send_edges(1)
        late_copy().start()

    fill_rows(1)
    send_rows(1)

    fill_base(1, base, out)

    add_ghost(1, out)

    @pl.when(outer)
    def _():
        for b in range(SPANS):
            cols = slice(b * WIDE, (b + 1) * WIDE)
            out[FORCED, :, cols] = out[FORCED, :, cols] + forcing[b * ROWS:(b + 1) * ROWS]

    take_rows(1)
    for piece, (start, stop) in enumerate(PIECES):
        take_layers(1, piece)
        for f in range(FIELDS):
            out[f, :, start:stop] = with_halos(out[f, :, start:stop], 1, f, start, stop)

    @pl.when(z == LAYERS - 2)
    def _():
        late_copy().wait_recv()
        out[FORCED] = out[FORCED] + late_in[...]

    for step in range(2):
        edges_moved(step).wait_send()
        for way, flag in ((0, has_high), (1, has_low)):
            @pl.when(flag)
            def _():
                layer_copy(step, way).wait_send()

        for way, flag in ((0, has_south), (1, has_north)):
            @pl.when(flag)
            def _():
                row_copy(step, way).wait_send()

    obs1_moved().wait_send()
    obs2_moved().wait_send()

    @pl.when(inner)
    def _():
        obs3_copy().wait_send()

    @pl.when(outer)
    def _():
        late_copy().wait_send()


def steps(*operands):
    dma = pltpu.SemaphoreType.DMA
    state = (FIELDS, ROWS, COLS)
    terms = 2 * POINTS * EDGE
    pairs = LINES // 2
    inputs = [
        pltpu.SMEM(x.shape, x.dtype) if i in (2, 3) else pltpu.VMEM(x.shape, x.dtype)
        for i, x in enumerate(operands)
    ]
    return pl.pallas_call(
        kernel,
        out_shape=jax.ShapeDtypeStruct(state, F32),
        in_specs=[pl.BlockSpec(memory_space=pltpu.HBM)] * len(operands),
        out_specs=pl.BlockSpec(memory_space=pltpu.VMEM),
        scratch_shapes=inputs + [
            dma((len(operands),)),
            pltpu.VMEM(state, F32),
            pltpu.VMEM(state, F32),
            pltpu.VMEM(state[1:], F32),
            pltpu.VMEM(state, F32),
            pltpu.VMEM((2, 2) + state, F32),
            pltpu.VMEM((2, 2, FIELDS, COLS), F32),
            pltpu.VMEM((2, 2, FIELDS, COLS), F32),
            pltpu.VMEM((2, 1, LANES), F32),
            pltpu.VMEM((2, TILES, LANES), F32),
            pltpu.VMEM((2, 8, EDGE), F32),
            pltpu.VMEM((HIGH, terms), BF16),
            pltpu.VMEM((WIDE, terms), BF16),
            pltpu.VMEM((2 * FIELDS * HIGH, terms), BF16),
            pltpu.VMEM((TILES, 4, LANES), F32),
            pltpu.VMEM((LINES, GROUP, 4, LANES), F32),
            pltpu.VMEM((GROUP, pairs, 4, LANES), F32),
            pltpu.VMEM((GROUP, pairs, 4, LANES), F32),
            pltpu.VMEM((LAYERS, GROUP, pairs, 4, LANES), F32),
            pltpu.VMEM((2 * HIGH, WIDE), F32),
            pltpu.VMEM(state[1:], F32),
            pltpu.VMEM(state[1:], F32),
            dma((2, 2)), dma((2, 2, len(PIECES))),
            dma((2, 2)), dma((2, 2)),
            dma((2,)), dma((2,)),
            dma((3,)), dma((4,)),
            dma(()), dma(()), pltpu.SemaphoreType.REGULAR,
        ],
        compiler_params=pltpu.CompilerParams(
            collective_id=0, has_side_effects=True, vmem_limit_bytes=60 << 20
        ),
        name="adjoint_steps",
    )(*operands)


def body(
    adj_final, cond, diffus, couple, ghost_row, ghost_col, ghost_wt, obs_dest, obs_cell, obs_wt,
    misfit,
):
    final = steps(
        adj_final.reshape(FIELDS, ROWS, COLS), cond[0, 0], diffus, couple, ghost_row, ghost_col,
        ghost_wt, obs_dest.reshape(1, OBS), obs_cell[0, 0], obs_wt[0, 0], misfit[0, 0],
    )
    return final[None, :, None]


def solution(mesh):
    placed = (
        P("panel", None, "rad", "ang", None),
        P("panel", "rad", "ang", None),
        P(),
        P(),
        P(),
        P(),
        P(),
        P("panel", "rad", "ang", None),
        P("panel", "rad", None, "ang"),
        P("panel", "rad", None, "ang"),
        P("panel", "rad", None, "ang"),
    )
    return jax.shard_map(
        body,
        mesh=mesh,
        in_specs=placed,
        out_specs=P("panel", None, "rad", "ang", None),
        check_vma=False,
    )
```

```python
import functools
import jax
import jax.numpy as jnp
from jax import lax
from jax.experimental import pallas as pl
from jax.experimental.pallas import tpu as pltpu
from jax.sharding import PartitionSpec as P

MESH = pl.DeviceIdType.MESH
F32, BF16 = jnp.float32, jnp.bfloat16
FIELDS, ROWS, COLS = 7, 8, 1536
LANES = 128
BLOCKS = COLS // LANES
WIDE = 256
SPANS = COLS // WIDE
HIGH = ROWS * SPANS
LAYERS, TILES, GROUP = 8, 32, 4
LINES = TILES // GROUP
HALF = LAYERS // 2
SLOTS = 16
POINTS = 4
OBS = 256
EDGE = TILES * ROWS
FORCED = 3

PIECES = ((0, 128), (1408, 1536), (128, 768), (768, 1408))
EDGE_PIECES = 2


def iota(shape, dim, dtype=jnp.int32):
    value = lax.broadcasted_iota(jnp.int32, shape, dim)
    return value if dtype == jnp.int32 else value.astype(dtype)


def dot_rows(a, b, precision=None):
    return lax.dot_general(
        a, b, (((1,), (1,)), ((), ())), precision=precision, preferred_element_type=F32
    )


def indicator(count, row):
    small = row.astype(BF16)
    hot = iota((count, row.shape[1]), 0, F32).astype(BF16) == jnp.broadcast_to(small, (count, row.shape[1]))
    return jnp.where(hot, jnp.ones((), BF16), jnp.zeros((), BF16))


def spread(high_hot, row):
    count, width = high_hot.shape
    wide = jnp.broadcast_to(row, (16, width))
    top = wide.astype(BF16)
    rest = (wide - top.astype(F32)).astype(BF16)
    grid = high_hot.reshape(count // 16, 16, width)
    return [(grid * part[None]).reshape(count, width) for part in (top, rest)]


def kernel(
    adj_hbm, cond_hbm, diffus_hbm, couple_hbm, ghost_row_hbm, ghost_col_hbm, ghost_wt_hbm,
    dest_hbm, cell_hbm, obs_wt_hbm, misfit_hbm,
    out,
    adj, cond, diffus, couple, ghost_row, ghost_col, ghost_wt, dest, cell, obs_wt, misfit, load_s,
    scaled_a, scaled_b, scaled_f, base, layer_in, row_out, row_in,
    edge_out, edge_all, edge_rows,
    high_hot, low_hot, spread_rows,
    outbox, line_in, pair_sum, tile_in, forced_in, forcing, late_out, late_in,
    layer_ss, layer_rs, row_ss, row_rs,
    edge_ss, edge_rs, obs_ss, obs_rs, late_ss, late_rs, open_s,
):
    loads = [
        pltpu.make_async_copy(source, target, load_s.at[i])
        for i, (source, target) in enumerate((
            (adj_hbm, adj), (cond_hbm, cond), (diffus_hbm, diffus), (couple_hbm, couple),
            (dest_hbm, dest), (cell_hbm, cell), (obs_wt_hbm, obs_wt), (misfit_hbm, misfit),
            (ghost_row_hbm, ghost_row), (ghost_col_hbm, ghost_col), (ghost_wt_hbm, ghost_wt),
        ))
    ]
    for load in loads[:3]:
        load.start()

    p, z, a = lax.axis_index("panel"), lax.axis_index("rad"), lax.axis_index("ang")
    y, q = a // GROUP, lax.rem(a, GROUP)
    has_low, has_high = z > 0, z < LAYERS - 1
    has_north, has_south = a > 0, a < TILES - 1
    outer = z == LAYERS - 1
    inner = z < LAYERS - 1
    scaled = (scaled_a, scaled_b)

    def along_line(step):
        return lax.rem(y + step, LINES)

    def beside(step):
        return lax.rem(q + step, GROUP)

    barrier = pltpu.get_barrier_semaphore()

    def greet(panel, layer, tile):
        pl.semaphore_signal(barrier, inc=1, device_id=(panel, layer, tile), device_id_type=MESH)

    order = sorted(range(TILES), key=lambda i: -min(i, TILES - i))
    for i in order:
        greet(1 - p, z, lax.rem(a + i, TILES))
    for i in sorted(range(1, LINES), key=lambda i: -min(i, LINES - i)):
        greet(p, z, along_line(i) * GROUP + q)

    @pl.when(has_low)
    def _():
        greet(p, z - 1, a)

    @pl.when(has_high)
    def _():
        greet(p, z + 1, a)

    @pl.when(has_north)
    def _():
        greet(p, z, a - 1)

    @pl.when(has_south)
    def _():
        greet(p, z, a + 1)

    for i in range(1, GROUP):
        greet(p, z, y * GROUP + beside(i))

    @pl.when(inner)
    def _():
        greet(p, LAYERS - 1, a)

    for load in loads[3:]:
        load.start()

    def remote(source, target, send, recv, device):
        return pltpu.make_async_remote_copy(
            src_ref=source, dst_ref=target, send_sem=send, recv_sem=recv,
            device_id=device, device_id_type=MESH,
        )

    def layer_copy(step, way, start=0, stop=COLS, piece=0):
        return remote(
            scaled[step].at[:, :, start:stop], layer_in.at[step, way, :, :, start:stop],
            layer_ss.at[step, way], layer_rs.at[step, way, piece],
            (p, z + 1 if way == 0 else z - 1, a),
        )

    def row_copy(step, way):
        return remote(
            row_out.at[step, way], row_in.at[step, way], row_ss.at[step, way], row_rs.at[step, way],
            (p, z, a + 1 if way == 0 else a - 1),
        )

    def edge_copy(step, i):
        return remote(
            edge_out.at[step], edge_all.at[step, pl.ds(a, 1), :], edge_ss.at[step], edge_rs.at[step],
            (1 - p, z, lax.rem(a + i, TILES)),
        )

    def edges_moved(step):
        everything = edge_all.at[step]
        return remote(everything, everything, edge_ss.at[step], edge_rs.at[step], (1 - p, z, a))

    def obs1_copy(i):
        target = along_line(i)
        return remote(
            outbox.at[pl.ds(target * GROUP, GROUP)], line_in.at[y], obs_ss.at[0], obs_rs.at[0],
            (p, z, target * GROUP + q),
        )

    def obs1_moved():
        others = line_in.at[pl.ds(0, LINES - 1)]
        return remote(others, others, obs_ss.at[0], obs_rs.at[0], (1 - p, z, a))

    def obs2_copy(i):
        target = beside(i)
        return remote(
            pair_sum.at[target], tile_in.at[q], obs_ss.at[1], obs_rs.at[1],
            (p, z, y * GROUP + target),
        )

    def obs2_moved():
        others = tile_in.at[pl.ds(0, GROUP - 1)]
        return remote(others, others, obs_ss.at[1], obs_rs.at[1], (1 - p, z, a))

    def obs3_copy():
        return remote(
            tile_in, forced_in.at[z], obs_ss.at[2], obs_rs.at[2 + z // HALF], (p, LAYERS - 1, a)
        )

    def obs3_moved(start, count):
        others = forced_in.at[pl.ds(start, count)]
        return remote(
            others, others, obs_ss.at[2], obs_rs.at[2 + start // HALF], (1 - p, z, a)
        )

    def late_copy():
        return remote(late_out, late_in, late_ss, late_rs, (p, z - 1, a))

    def send_layers(step, piece):
        start, stop = PIECES[piece]

        @pl.when(has_high)
        def _():
            layer_copy(step, 0, start, stop, piece).start()

        @pl.when(has_low)
        def _():
            layer_copy(step, 1, start, stop, piece).start()

    def take_layers(step, piece):
        start, stop = PIECES[piece]

        @pl.when(has_low)
        def _():
            layer_copy(step, 0, start, stop, piece).wait_recv()

        @pl.when(has_high)
        def _():
            layer_copy(step, 1, start, stop, piece).wait_recv()

    def send_rows(step):
        @pl.when(has_south)
        def _():
            row_copy(step, 0).start()

        @pl.when(has_north)
        def _():
            row_copy(step, 1).start()

    def take_rows(step):
        @pl.when(has_north)
        def _():
            row_copy(step, 0).wait_recv()

        @pl.when(has_south)
        def _():
            row_copy(step, 1).wait_recv()

    def field_of(step, f):
        return scaled_f if step == 1 and f == FORCED else scaled[step].at[f]

    runs = LANES // ROWS
    lane_of = iota((ROWS, LANES), 1)
    own_run = jnp.where(
        lax.rem(lane_of, ROWS) == iota((ROWS, LANES), 0),
        lax.rem(lane_of // ROWS - lax.rem(a, runs) + runs, runs), -1,
    )
    sent_run = lax.rem(iota((runs, LANES), 1) // ROWS - iota((runs, LANES), 0) + runs, runs)

    def fill_rows(step):
        for f in range(FIELDS):
            row_out[step, 0, f:f + 1, :] = field_of(step, f)[ROWS - 1:ROWS, :]
            row_out[step, 1, f:f + 1, :] = field_of(step, f)[0:1, :]

    def fill_edges(step):
        wide = jnp.zeros((ROWS, LANES), F32)
        for f in range(FIELDS):
            for side, at in ((0, 0), (1, COLS - 1)):
                start = at // LANES * LANES
                block = field_of(step, f)[:, start:start + LANES]
                column = block[:, at - start:at - start + 1]
                wide = jnp.where(
                    own_run == 2 * f + side, jnp.broadcast_to(column, (ROWS, LANES)), wide
                )
        edge_out[step] = jnp.sum(wide, axis=0, keepdims=True)

    def send_edges(step):
        fill_edges(step)
        for i in order:
            edge_copy(step, i).start()

    def fill_base(step, source, target):
        rate = [[couple[e, c] for c in range(FIELDS)] for e in range(FIELDS)]
        for b in range(BLOCKS):
            cols = slice(b * LANES, (b + 1) * LANES)
            state = [source[e, :, cols] for e in range(FIELDS)]
            for c in range(FIELDS):
                total = state[c]
                for e in range(FIELDS):
                    total = total + rate[e][c] * state[e]
                target[c, :, cols] = total
        col_of = iota((ROWS, COLS), 1)
        row_of = iota((ROWS, COLS), 0)
        for f in range(FIELDS):
            s = field_of(step, f)[...]
            west = jnp.where(col_of == 0, 0.0, pltpu.roll(s, 1, 1))
            east = jnp.where(col_of == COLS - 1, 0.0, pltpu.roll(s, COLS - 1, 1))
            north = jnp.where(row_of == 0, 0.0, pltpu.roll(s, 1, 0))
            south = jnp.where(row_of == ROWS - 1, 0.0, pltpu.roll(s, ROWS - 1, 0))
            target[f] = target[f] + ((west + east) + (north + south) - 6.0 * s)

    def add_ghost(step, target):
        edges_moved(step).wait_recv()
        for f in range(FIELDS):
            for side in range(2):
                run = 2 * f + side
                for h in range(2):
                    part = jnp.where(
                        sent_run == run, edge_all[step, h * runs:(h + 1) * runs, :], 0.0
                    )
                    line = jnp.sum(part, axis=0, keepdims=True)
                    if run:
                        line = pltpu.roll(line, LANES - ROWS * run, 1)
                    edge_rows[side, f:f + 1, h * LANES:(h + 1) * LANES] = line
        for f in range(FIELDS):
            rows = [
                edge_rows[side, f:f + 1, :] * ghost_wt[side, point:point + 1, :]
                for side in range(2) for point in range(POINTS)
            ]
            top, rest = spread(high_hot[...], jnp.concatenate(rows, axis=1))
            spread_rows[f * HIGH:(f + 1) * HIGH] = top
            spread_rows[(FIELDS + f) * HIGH:(FIELDS + f + 1) * HIGH] = rest
        cells = dot_rows(spread_rows[...], low_hot[...])
        for f in range(FIELDS):
            for b in range(SPANS):
                at = f * HIGH + b * ROWS
                more = at + FIELDS * HIGH
                cols = slice(b * WIDE, (b + 1) * WIDE)
                target[f, :, cols] = target[f, :, cols] + (
                    cells[at:at + ROWS] + cells[more:more + ROWS]
                )

    for load in loads[:3]:
        load.wait()
    for f in range(FIELDS):
        scaled_a[f] = (diffus[f] * cond[...]) * adj[f]

    fill_edges(0)
    fill_rows(0)

    for load in loads[3:]:
        load.wait()
    owner_hot = jnp.where(iota((TILES, OBS), 0) == dest[...], 1.0, 0.0)
    earlier = jnp.where(iota((OBS, OBS), 1) < iota((OBS, OBS), 0), 1.0, 0.0).astype(BF16)
    before = dot_rows(owner_hot.astype(BF16), earlier)
    rank = jnp.sum(owner_hot * before, axis=0, keepdims=True)
    in_slot = rank == iota((SLOTS, OBS), 0, F32)
    number = cell[...]
    in_row = jnp.floor((number.astype(F32) + 0.5) * (1.0 / COLS)).astype(jnp.int32)
    column = number - in_row * COLS
    place = (
        (lax.shift_right_logical(column, 8) * ROWS + in_row) * WIDE + (column & (WIDE - 1))
    ).astype(F32)
    payload = []
    for kind in range(3):
        for point in range(POINTS):
            if kind < 2:
                row = misfit[kind:kind + 1, :] * obs_wt[point:point + 1, :]
            else:
                row = place[point:point + 1, :]
            payload.append(jnp.where(in_slot, jnp.broadcast_to(row, (SLOTS, OBS)), 0.0))
    packed = dot_rows(owner_hot, jnp.concatenate(payload, axis=0), lax.Precision.HIGHEST)
    width = SLOTS * POINTS
    own_half = iota((TILES, LANES), 1) // width == lax.rem(y, 2)
    for kind in range(3):
        part = packed[:, kind * width:(kind + 1) * width]
        outbox[:, kind, :] = jnp.where(own_half, jnp.concatenate([part, part], axis=1), 0.0)
    outbox[:, 3, :] = jnp.zeros((TILES, LANES), F32)
    for side in range(2):
        for point in range(POINTS):
            at = (side * POINTS + point) * EDGE
            local = ghost_row[side, point:point + 1, :] - a * ROWS
            col = ghost_col[side, point:point + 1, :]
            inside = (local >= 0) & (local < ROWS)
            high = jnp.where(inside, lax.shift_right_logical(col, 8) * ROWS + local, -1)
            low = col & (WIDE - 1)
            high_hot[:, at:at + EDGE] = indicator(HIGH, high.astype(F32))
            low_hot[:, at:at + EDGE] = indicator(WIDE, low.astype(F32))

    def count(flag):
        return jnp.where(flag, 1, 0)

    expected = (
        TILES + LINES - 1 + GROUP - 1
        + count(has_low) + count(has_high) + count(has_north) + count(has_south)
        + jnp.where(outer, LAYERS - 1, 0)
    )
    pl.semaphore_wait(barrier, expected)

    @pl.when(outer)
    def _():
        for i in range(LAYERS - 1):
            pl.semaphore_signal(open_s, inc=1, device_id=(p, i, a), device_id_type=MESH)

    for i in range(1, LINES):
        obs1_copy(i).start()
    line_in[y] = outbox[pl.ds(y * GROUP, GROUP)]

    for i in order:
        edge_copy(0, i).start()
    for piece in range(len(PIECES)):
        send_layers(0, piece)
    send_rows(0)

    obs1_moved().wait_recv()
    for i in range(GROUP):
        for pair in range(LINES // 2):
            pair_sum[i, pair] = line_in[2 * pair, i] + line_in[2 * pair + 1, i]
    for i in range(1, GROUP):
        obs2_copy(i).start()
    tile_in[q] = pair_sum[q]

    for step in range(2):
        @pl.when(jnp.logical_not(has_low))
        def _():
            layer_in[step, 0] = jnp.zeros((FIELDS, ROWS, COLS), F32)

        @pl.when(jnp.logical_not(has_high))
        def _():
            layer_in[step, 1] = jnp.zeros((FIELDS, ROWS, COLS), F32)

        @pl.when(jnp.logical_not(has_north))
        def _():
            row_in[step, 0] = jnp.zeros((FIELDS, COLS), F32)

        @pl.when(jnp.logical_not(has_south))
        def _():
            row_in[step, 1] = jnp.zeros((FIELDS, COLS), F32)

    fill_base(0, adj, base)
    obs2_moved().wait_recv()

    def send_third(flag):
        @pl.when(flag)
        def _():
            pl.semaphore_wait(open_s, 1)
            obs3_copy().start()

    send_third(inner & (z >= 2))

    add_ghost(0, base)

    def one_layer(layer, carry):
        rows = [[], [], []]
        for i in range(GROUP):
            for pair in range(LINES // 2):
                for kind in range(3):
                    rows[kind].append(forced_in[layer, i, pair, kind:kind + 1, :])
        early, late, places = [jnp.concatenate(r, axis=1) for r in rows]
        high = jnp.floor(places * (1.0 / WIDE))
        hot_high = indicator(HIGH, high)
        hot_low = indicator(WIDE, places - high * WIDE)
        top_a, rest_a = spread(hot_high, early)
        top_b, rest_b = spread(hot_high, late)
        cells = dot_rows(jnp.concatenate([top_a, top_b, rest_a, rest_b], axis=0), hot_low)
        forcing[...] = forcing[...] + (cells[:2 * HIGH] + cells[2 * HIGH:])
        return carry

    @pl.when(outer)
    def _():
        forcing[...] = jnp.zeros((2 * HIGH, WIDE), F32)
        obs3_moved(0, HALF).wait_recv()
        lax.fori_loop(0, HALF, one_layer, 0, unroll=2)

    def with_halos(value, step, f, start, stop):
        size = stop - start
        row_of = iota((ROWS, size), 0)
        value = value + (layer_in[step, 0, f, :, start:stop] + layer_in[step, 1, f, :, start:stop])
        north = jnp.broadcast_to(row_in[step, 0, f:f + 1, start:stop], (ROWS, size))
        south = jnp.broadcast_to(row_in[step, 1, f:f + 1, start:stop], (ROWS, size))
        return value + jnp.where(row_of == 0, north, jnp.where(row_of == ROWS - 1, south, 0.0))

    take_rows(0)
    for piece, (start, stop) in enumerate(PIECES):
        take_layers(0, piece)
        for f in range(FIELDS):
            value = with_halos(base[f, :, start:stop], 0, f, start, stop)
            base[f, :, start:stop] = value
            scaled_b[f, :, start:stop] = (diffus[f] * cond[:, start:stop]) * value
        send_layers(1, piece)
        if piece == EDGE_PIECES - 1:
            scaled_f[:, :LANES] = scaled_b[FORCED, :, :LANES]
            scaled_f[:, COLS - LANES:] = scaled_b[FORCED, :, COLS - LANES:]

            @pl.when(inner)
            def _():
                send_edges(1)

            send_third(z < 2)
    scaled_f[...] = scaled_b[FORCED]

    @pl.when(outer)
    def _():
        forced_in[LAYERS - 1] = tile_in[...]
        obs3_moved(HALF, HALF - 1).wait_recv()
        lax.fori_loop(HALF, LAYERS, one_layer, 0, unroll=2)
        for b in range(SPANS):
            cols = slice(b * WIDE, (b + 1) * WIDE)
            added = forcing[HIGH + b * ROWS:HIGH + (b + 1) * ROWS]
            share = (diffus[FORCED] * cond[:, cols]) * added
            base[FORCED, :, cols] = base[FORCED, :, cols] + added
            scaled_f[:, cols] = scaled_f[:, cols] + share
            late_out[:, cols] = share
        send_edges(1)
        late_copy().start()

    fill_rows(1)
    send_rows(1)

    fill_base(1, base, out)

    add_ghost(1, out)

    @pl.when(outer)
    def _():
        for b in range(SPANS):
            cols = slice(b * WIDE, (b + 1) * WIDE)
            out[FORCED, :, cols] = out[FORCED, :, cols] + forcing[b * ROWS:(b + 1) * ROWS]

    take_rows(1)
    for piece, (start, stop) in enumerate(PIECES):
        take_layers(1, piece)
        for f in range(FIELDS):
            out[f, :, start:stop] = with_halos(out[f, :, start:stop], 1, f, start, stop)

    @pl.when(z == LAYERS - 2)
    def _():
        late_copy().wait_recv()
        out[FORCED] = out[FORCED] + late_in[...]

    for step in range(2):
        edges_moved(step).wait_send()
        for way, flag in ((0, has_high), (1, has_low)):
            @pl.when(flag)
            def _():
                layer_copy(step, way).wait_send()

        for way, flag in ((0, has_south), (1, has_north)):
            @pl.when(flag)
            def _():
                row_copy(step, way).wait_send()

    obs1_moved().wait_send()
    obs2_moved().wait_send()

    @pl.when(inner)
    def _():
        obs3_copy().wait_send()

    @pl.when(outer)
    def _():
        late_copy().wait_send()


def steps(*operands):
    dma = pltpu.SemaphoreType.DMA
    state = (FIELDS, ROWS, COLS)
    terms = 2 * POINTS * EDGE
    pairs = LINES // 2
    inputs = [
        pltpu.SMEM(x.shape, x.dtype) if i in (2, 3) else pltpu.VMEM(x.shape, x.dtype)
        for i, x in enumerate(operands)
    ]
    return pl.pallas_call(
        kernel,
        out_shape=pltpu.VMEM(state, F32),
        in_specs=[pl.BlockSpec(memory_space=pltpu.HBM)] * len(operands),
        out_specs=pl.BlockSpec(memory_space=pltpu.VMEM),
        scratch_shapes=inputs + [
            dma((len(operands),)),
            pltpu.VMEM(state, F32),
            pltpu.VMEM(state, F32),
            pltpu.VMEM(state[1:], F32),
            pltpu.VMEM(state, F32),
            pltpu.VMEM((2, 2) + state, F32),
            pltpu.VMEM((2, 2, FIELDS, COLS), F32),
            pltpu.VMEM((2, 2, FIELDS, COLS), F32),
            pltpu.VMEM((2, 1, LANES), F32),
            pltpu.VMEM((2, TILES, LANES), F32),
            pltpu.VMEM((2, 8, EDGE), F32),
            pltpu.VMEM((HIGH, terms), BF16),
            pltpu.VMEM((WIDE, terms), BF16),
            pltpu.VMEM((2 * FIELDS * HIGH, terms), BF16),
            pltpu.VMEM((TILES, 4, LANES), F32),
            pltpu.VMEM((LINES, GROUP, 4, LANES), F32),
            pltpu.VMEM((GROUP, pairs, 4, LANES), F32),
            pltpu.VMEM((GROUP, pairs, 4, LANES), F32),
            pltpu.VMEM((LAYERS, GROUP, pairs, 4, LANES), F32),
            pltpu.VMEM((2 * HIGH, WIDE), F32),
            pltpu.VMEM(state[1:], F32),
            pltpu.VMEM(state[1:], F32),
            dma((2, 2)), dma((2, 2, len(PIECES))),
            dma((2, 2)), dma((2, 2)),
            dma((2,)), dma((2,)),
            dma((3,)), dma((4,)),
            dma(()), dma(()), pltpu.SemaphoreType.REGULAR,
        ],
        compiler_params=pltpu.CompilerParams(
            collective_id=0, has_side_effects=True, vmem_limit_bytes=61440 << 10
        ),
        name="adjoint_steps",
    )(*operands)


def body(
    adj_final, cond, diffus, couple, ghost_row, ghost_col, ghost_wt, obs_dest, obs_cell, obs_wt,
    misfit,
):
    final = steps(
        adj_final.reshape(FIELDS, ROWS, COLS), cond[0, 0], diffus, couple, ghost_row, ghost_col,
        ghost_wt, obs_dest.reshape(1, OBS), obs_cell[0, 0], obs_wt[0, 0], misfit[0, 0],
    )
    return final[None, :, None]


def solution(mesh):
    placed = (
        P("panel", None, "rad", "ang", None),
        P("panel", "rad", "ang", None),
        P(),
        P(),
        P(),
        P(),
        P(),
        P("panel", "rad", "ang", None),
        P("panel", "rad", None, "ang"),
        P("panel", "rad", None, "ang"),
        P("panel", "rad", None, "ang"),
    )
    return jax.shard_map(
        body,
        mesh=mesh,
        in_specs=placed,
        out_specs=P("panel", None, "rad", "ang", None),
        check_vma=False,
    )
```

```python
import functools
import jax
import jax.numpy as jnp
from jax import lax
from jax.experimental import pallas as pl
from jax.experimental.pallas import tpu as pltpu
from jax.sharding import PartitionSpec as P

MESH = pl.DeviceIdType.MESH
F32, BF16 = jnp.float32, jnp.bfloat16
FIELDS, ROWS, COLS = 7, 8, 1536
LANES = 128
BLOCKS = COLS // LANES
WIDE = 256
SPANS = COLS // WIDE
HIGH = ROWS * SPANS
LAYERS, TILES, GROUP = 8, 32, 4
LINES = TILES // GROUP
HALF = LAYERS // 2
SLOTS = 16
POINTS = 4
OBS = 256
EDGE = TILES * ROWS
FORCED = 3

PIECES = ((0, 128), (1408, 1536), (128, 768), (768, 1408))
EDGE_PIECES = 2


def iota(shape, dim, dtype=jnp.int32):
    value = lax.broadcasted_iota(jnp.int32, shape, dim)
    return value if dtype == jnp.int32 else value.astype(dtype)


def dot_rows(a, b, precision=None):
    return lax.dot_general(
        a, b, (((1,), (1,)), ((), ())), precision=precision, preferred_element_type=F32
    )


def indicator(count, row):
    small = row.astype(BF16)
    hot = iota((count, row.shape[1]), 0, F32).astype(BF16) == jnp.broadcast_to(small, (count, row.shape[1]))
    return jnp.where(hot, jnp.ones((), BF16), jnp.zeros((), BF16))


def spread(high_hot, row):
    count, width = high_hot.shape
    wide = jnp.broadcast_to(row, (16, width))
    top = wide.astype(BF16)
    rest = (wide - top.astype(F32)).astype(BF16)
    grid = high_hot.reshape(count // 16, 16, width)
    return [(grid * part[None]).reshape(count, width) for part in (top, rest)]


def kernel(
    adj_hbm, cond_hbm, diffus_hbm, couple_hbm, ghost_row_hbm, ghost_col_hbm, ghost_wt_hbm,
    dest_hbm, cell_hbm, obs_wt_hbm, misfit_hbm,
    out,
    adj, cond, diffus, couple, ghost_row, ghost_col, ghost_wt, dest, cell, obs_wt, misfit, load_s,
    scaled_a, scaled_b, scaled_f, base, layer_in, row_out, row_in,
    edge_out, edge_all, edge_rows,
    high_hot, low_hot, spread_rows,
    outbox, line_in, tile_in, forced_in, forcing, late_out, late_in,
    layer_ss, layer_rs, row_ss, row_rs,
    edge_ss, edge_rs, obs_ss, obs_rs, late_ss, late_rs, open_s,
):
    loads = [
        pltpu.make_async_copy(source, target, load_s.at[i])
        for i, (source, target) in enumerate((
            (adj_hbm, adj), (cond_hbm, cond), (diffus_hbm, diffus), (couple_hbm, couple),
            (dest_hbm, dest), (cell_hbm, cell), (obs_wt_hbm, obs_wt), (misfit_hbm, misfit),
            (ghost_row_hbm, ghost_row), (ghost_col_hbm, ghost_col), (ghost_wt_hbm, ghost_wt),
        ))
    ]
    for load in loads[:3]:
        load.start()

    p, z, a = lax.axis_index("panel"), lax.axis_index("rad"), lax.axis_index("ang")
    y, q = a // GROUP, lax.rem(a, GROUP)
    has_low, has_high = z > 0, z < LAYERS - 1
    has_north, has_south = a > 0, a < TILES - 1
    outer = z == LAYERS - 1
    inner = z < LAYERS - 1
    scaled = (scaled_a, scaled_b)

    barrier = pltpu.get_barrier_semaphore()

    def greet(panel, layer, tile):
        pl.semaphore_signal(barrier, inc=1, device_id=(panel, layer, tile), device_id_type=MESH)

    order = sorted(range(TILES), key=lambda i: -min(i, TILES - i))
    for i in order:
        greet(1 - p, z, lax.rem(a + i, TILES))
        if i:
            greet(p, z, lax.rem(a + i, TILES))

    @pl.when(has_low)
    def _():
        greet(p, z - 1, a)

    @pl.when(has_high)
    def _():
        greet(p, z + 1, a)

    @pl.when(has_north)
    def _():
        greet(p, z, a - 1)

    @pl.when(has_south)
    def _():
        greet(p, z, a + 1)


    @pl.when(inner)
    def _():
        greet(p, LAYERS - 1, a)

    for load in loads[3:]:
        load.start()

    def remote(source, target, send, recv, device):
        return pltpu.make_async_remote_copy(
            src_ref=source, dst_ref=target, send_sem=send, recv_sem=recv,
            device_id=device, device_id_type=MESH,
        )

    def layer_copy(step, way, start=0, stop=COLS, piece=0):
        return remote(
            scaled[step].at[:, :, start:stop], layer_in.at[step, way, :, :, start:stop],
            layer_ss.at[step, way], layer_rs.at[step, way, piece],
            (p, z + 1 if way == 0 else z - 1, a),
        )

    def row_copy(step, way):
        return remote(
            row_out.at[step, way], row_in.at[step, way], row_ss.at[step, way], row_rs.at[step, way],
            (p, z, a + 1 if way == 0 else a - 1),
        )

    def edge_copy(step, i):
        return remote(
            edge_out.at[step], edge_all.at[step, pl.ds(a, 1), :], edge_ss.at[step], edge_rs.at[step],
            (1 - p, z, lax.rem(a + i, TILES)),
        )

    def edges_moved(step):
        everything = edge_all.at[step]
        return remote(everything, everything, edge_ss.at[step], edge_rs.at[step], (1 - p, z, a))

    def obs1_copy(i):
        target = lax.rem(a + i, TILES)
        return remote(
            outbox.at[target], line_in.at[a], obs_ss.at[0], obs_rs.at[0], (p, z, target)
        )

    def obs1_moved():
        others = line_in.at[pl.ds(0, TILES - 1)]
        return remote(others, others, obs_ss.at[0], obs_rs.at[0], (1 - p, z, a))

    def obs3_copy():
        return remote(
            tile_in, forced_in.at[z], obs_ss.at[2], obs_rs.at[2 + z // HALF], (p, LAYERS - 1, a)
        )

    def obs3_moved(start, count):
        others = forced_in.at[pl.ds(start, count)]
        return remote(
            others, others, obs_ss.at[2], obs_rs.at[2 + start // HALF], (1 - p, z, a)
        )

    def late_copy():
        return remote(late_out, late_in, late_ss, late_rs, (p, z - 1, a))

    def send_layers(step, piece):
        start, stop = PIECES[piece]

        @pl.when(has_high)
        def _():
            layer_copy(step, 0, start, stop, piece).start()

        @pl.when(has_low)
        def _():
            layer_copy(step, 1, start, stop, piece).start()

    def take_layers(step, piece):
        start, stop = PIECES[piece]

        @pl.when(has_low)
        def _():
            layer_copy(step, 0, start, stop, piece).wait_recv()

        @pl.when(has_high)
        def _():
            layer_copy(step, 1, start, stop, piece).wait_recv()

    def send_rows(step):
        @pl.when(has_south)
        def _():
            row_copy(step, 0).start()

        @pl.when(has_north)
        def _():
            row_copy(step, 1).start()

    def take_rows(step):
        @pl.when(has_north)
        def _():
            row_copy(step, 0).wait_recv()

        @pl.when(has_south)
        def _():
            row_copy(step, 1).wait_recv()

    def field_of(step, f):
        return scaled_f if step == 1 and f == FORCED else scaled[step].at[f]

    runs = LANES // ROWS
    lane_of = iota((ROWS, LANES), 1)
    own_run = jnp.where(
        lax.rem(lane_of, ROWS) == iota((ROWS, LANES), 0),
        lax.rem(lane_of // ROWS - lax.rem(a, runs) + runs, runs), -1,
    )
    sent_run = lax.rem(iota((runs, LANES), 1) // ROWS - iota((runs, LANES), 0) + runs, runs)

    def fill_rows(step):
        for f in range(FIELDS):
            row_out[step, 0, f:f + 1, :] = field_of(step, f)[ROWS - 1:ROWS, :]
            row_out[step, 1, f:f + 1, :] = field_of(step, f)[0:1, :]

    def fill_edges(step):
        wide = jnp.zeros((ROWS, LANES), F32)
        for f in range(FIELDS):
            for side, at in ((0, 0), (1, COLS - 1)):
                start = at // LANES * LANES
                block = field_of(step, f)[:, start:start + LANES]
                column = block[:, at - start:at - start + 1]
                wide = jnp.where(
                    own_run == 2 * f + side, jnp.broadcast_to(column, (ROWS, LANES)), wide
                )
        edge_out[step] = jnp.sum(wide, axis=0, keepdims=True)

    def send_edges(step):
        fill_edges(step)
        for i in order:
            edge_copy(step, i).start()

    def fill_base(step, source, target):
        rate = [[couple[e, c] for c in range(FIELDS)] for e in range(FIELDS)]
        for b in range(BLOCKS):
            cols = slice(b * LANES, (b + 1) * LANES)
            state = [source[e, :, cols] for e in range(FIELDS)]
            for c in range(FIELDS):
                total = state[c]
                for e in range(FIELDS):
                    total = total + rate[e][c] * state[e]
                target[c, :, cols] = total
        col_of = iota((ROWS, COLS), 1)
        row_of = iota((ROWS, COLS), 0)
        for f in range(FIELDS):
            s = field_of(step, f)[...]
            west = jnp.where(col_of == 0, 0.0, pltpu.roll(s, 1, 1))
            east = jnp.where(col_of == COLS - 1, 0.0, pltpu.roll(s, COLS - 1, 1))
            north = jnp.where(row_of == 0, 0.0, pltpu.roll(s, 1, 0))
            south = jnp.where(row_of == ROWS - 1, 0.0, pltpu.roll(s, ROWS - 1, 0))
            target[f] = target[f] + ((west + east) + (north + south) - 6.0 * s)

    def add_ghost(step, target):
        edges_moved(step).wait_recv()
        for f in range(FIELDS):
            for side in range(2):
                run = 2 * f + side
                for h in range(2):
                    part = jnp.where(
                        sent_run == run, edge_all[step, h * runs:(h + 1) * runs, :], 0.0
                    )
                    line = jnp.sum(part, axis=0, keepdims=True)
                    if run:
                        line = pltpu.roll(line, LANES - ROWS * run, 1)
                    edge_rows[side, f:f + 1, h * LANES:(h + 1) * LANES] = line
        for f in range(FIELDS):
            rows = [
                edge_rows[side, f:f + 1, :] * ghost_wt[side, point:point + 1, :]
                for side in range(2) for point in range(POINTS)
            ]
            top, rest = spread(high_hot[...], jnp.concatenate(rows, axis=1))
            spread_rows[f * HIGH:(f + 1) * HIGH] = top
            spread_rows[(FIELDS + f) * HIGH:(FIELDS + f + 1) * HIGH] = rest
        cells = dot_rows(spread_rows[...], low_hot[...])
        for f in range(FIELDS):
            for b in range(SPANS):
                at = f * HIGH + b * ROWS
                more = at + FIELDS * HIGH
                cols = slice(b * WIDE, (b + 1) * WIDE)
                target[f, :, cols] = target[f, :, cols] + (
                    cells[at:at + ROWS] + cells[more:more + ROWS]
                )

    for load in loads[:3]:
        load.wait()
    for f in range(FIELDS):
        scaled_a[f] = (diffus[f] * cond[...]) * adj[f]

    fill_edges(0)
    fill_rows(0)

    for load in loads[3:]:
        load.wait()
    owner_hot = jnp.where(iota((TILES, OBS), 0) == dest[...], 1.0, 0.0)
    earlier = jnp.where(iota((OBS, OBS), 1) < iota((OBS, OBS), 0), 1.0, 0.0).astype(BF16)
    before = dot_rows(owner_hot.astype(BF16), earlier)
    rank = jnp.sum(owner_hot * before, axis=0, keepdims=True)
    in_slot = rank == iota((SLOTS, OBS), 0, F32)
    number = cell[...]
    in_row = jnp.floor((number.astype(F32) + 0.5) * (1.0 / COLS)).astype(jnp.int32)
    column = number - in_row * COLS
    place = (
        (lax.shift_right_logical(column, 8) * ROWS + in_row) * WIDE + (column & (WIDE - 1))
    ).astype(F32)
    payload = []
    for kind in range(3):
        for point in range(POINTS):
            if kind < 2:
                row = misfit[kind:kind + 1, :] * obs_wt[point:point + 1, :]
            else:
                row = place[point:point + 1, :]
            payload.append(jnp.where(in_slot, jnp.broadcast_to(row, (SLOTS, OBS)), 0.0))
    packed = dot_rows(owner_hot, jnp.concatenate(payload, axis=0), lax.Precision.HIGHEST)
    width = SLOTS * POINTS
    own_half = iota((TILES, LANES), 1) // width == lax.rem(y, 2)
    for kind in range(3):
        part = packed[:, kind * width:(kind + 1) * width]
        outbox[:, kind, :] = jnp.where(own_half, jnp.concatenate([part, part], axis=1), 0.0)
    outbox[:, 3, :] = jnp.zeros((TILES, LANES), F32)
    for side in range(2):
        for point in range(POINTS):
            at = (side * POINTS + point) * EDGE
            local = ghost_row[side, point:point + 1, :] - a * ROWS
            col = ghost_col[side, point:point + 1, :]
            inside = (local >= 0) & (local < ROWS)
            high = jnp.where(inside, lax.shift_right_logical(col, 8) * ROWS + local, -1)
            low = col & (WIDE - 1)
            high_hot[:, at:at + EDGE] = indicator(HIGH, high.astype(F32))
            low_hot[:, at:at + EDGE] = indicator(WIDE, low.astype(F32))

    def count(flag):
        return jnp.where(flag, 1, 0)

    expected = (
        TILES + TILES - 1
        + count(has_low) + count(has_high) + count(has_north) + count(has_south)
        + jnp.where(outer, LAYERS - 1, 0)
    )
    pl.semaphore_wait(barrier, expected)

    @pl.when(outer)
    def _():
        for i in range(LAYERS - 1):
            pl.semaphore_signal(open_s, inc=1, device_id=(p, i, a), device_id_type=MESH)

    for i in order:
        if i:
            obs1_copy(i).start()
    line_in[a] = outbox[a]

    for i in order:
        edge_copy(0, i).start()
    for piece in range(len(PIECES)):
        send_layers(0, piece)
    send_rows(0)

    for step in range(2):
        @pl.when(jnp.logical_not(has_low))
        def _():
            layer_in[step, 0] = jnp.zeros((FIELDS, ROWS, COLS), F32)

        @pl.when(jnp.logical_not(has_high))
        def _():
            layer_in[step, 1] = jnp.zeros((FIELDS, ROWS, COLS), F32)

        @pl.when(jnp.logical_not(has_north))
        def _():
            row_in[step, 0] = jnp.zeros((FIELDS, COLS), F32)

        @pl.when(jnp.logical_not(has_south))
        def _():
            row_in[step, 1] = jnp.zeros((FIELDS, COLS), F32)

    fill_base(0, adj, base)
    obs1_moved().wait_recv()
    for i in range(GROUP):
        for pair in range(LINES // 2):
            tile = 2 * pair * GROUP + i
            tile_in[i, pair] = line_in[tile] + line_in[tile + GROUP]

    def send_third(flag):
        @pl.when(flag)
        def _():
            pl.semaphore_wait(open_s, 1)
            obs3_copy().start()

    send_third(inner & (z >= 2))

    add_ghost(0, base)

    def one_layer(layer, carry):
        rows = [[], [], []]
        for i in range(GROUP):
            for pair in range(LINES // 2):
                for kind in range(3):
                    rows[kind].append(forced_in[layer, i, pair, kind:kind + 1, :])
        early, late, places = [jnp.concatenate(r, axis=1) for r in rows]
        high = jnp.floor(places * (1.0 / WIDE))
        hot_high = indicator(HIGH, high)
        hot_low = indicator(WIDE, places - high * WIDE)
        top_a, rest_a = spread(hot_high, early)
        top_b, rest_b = spread(hot_high, late)
        cells = dot_rows(jnp.concatenate([top_a, top_b, rest_a, rest_b], axis=0), hot_low)
        forcing[...] = forcing[...] + (cells[:2 * HIGH] + cells[2 * HIGH:])
        return carry

    def with_halos(value, step, f, start, stop):
        size = stop - start
        row_of = iota((ROWS, size), 0)
        value = value + (layer_in[step, 0, f, :, start:stop] + layer_in[step, 1, f, :, start:stop])
        north = jnp.broadcast_to(row_in[step, 0, f:f + 1, start:stop], (ROWS, size))
        south = jnp.broadcast_to(row_in[step, 1, f:f + 1, start:stop], (ROWS, size))
        return value + jnp.where(row_of == 0, north, jnp.where(row_of == ROWS - 1, south, 0.0))

    take_rows(0)
    for piece, (start, stop) in enumerate(PIECES):
        take_layers(0, piece)
        for f in range(FIELDS):
            value = with_halos(base[f, :, start:stop], 0, f, start, stop)
            base[f, :, start:stop] = value
            scaled_b[f, :, start:stop] = (diffus[f] * cond[:, start:stop]) * value
        send_layers(1, piece)
        if piece == EDGE_PIECES - 1:
            scaled_f[:, :LANES] = scaled_b[FORCED, :, :LANES]
            scaled_f[:, COLS - LANES:] = scaled_b[FORCED, :, COLS - LANES:]

            @pl.when(inner)
            def _():
                send_edges(1)

            send_third(z < 2)
    scaled_f[...] = scaled_b[FORCED]

    @pl.when(outer)
    def _():
        forcing[...] = jnp.zeros((2 * HIGH, WIDE), F32)
        obs3_moved(0, HALF).wait_recv()
        lax.fori_loop(0, HALF, one_layer, 0, unroll=2)

    @pl.when(outer)
    def _():
        forced_in[LAYERS - 1] = tile_in[...]
        obs3_moved(HALF, HALF - 1).wait_recv()
        lax.fori_loop(HALF, LAYERS, one_layer, 0, unroll=2)
        for b in range(SPANS):
            cols = slice(b * WIDE, (b + 1) * WIDE)
            added = forcing[HIGH + b * ROWS:HIGH + (b + 1) * ROWS]
            share = (diffus[FORCED] * cond[:, cols]) * added
            base[FORCED, :, cols] = base[FORCED, :, cols] + added
            scaled_f[:, cols] = scaled_f[:, cols] + share
            late_out[:, cols] = share
        send_edges(1)
        late_copy().start()

    fill_rows(1)
    send_rows(1)

    fill_base(1, base, out)

    add_ghost(1, out)

    @pl.when(outer)
    def _():
        for b in range(SPANS):
            cols = slice(b * WIDE, (b + 1) * WIDE)
            out[FORCED, :, cols] = out[FORCED, :, cols] + forcing[b * ROWS:(b + 1) * ROWS]

    take_rows(1)
    for piece, (start, stop) in enumerate(PIECES):
        take_layers(1, piece)
        for f in range(FIELDS):
            out[f, :, start:stop] = with_halos(out[f, :, start:stop], 1, f, start, stop)

    @pl.when(z == LAYERS - 2)
    def _():
        late_copy().wait_recv()
        out[FORCED] = out[FORCED] + late_in[...]

    for step in range(2):
        edges_moved(step).wait_send()
        for way, flag in ((0, has_high), (1, has_low)):
            @pl.when(flag)
            def _():
                layer_copy(step, way).wait_send()

        for way, flag in ((0, has_south), (1, has_north)):
            @pl.when(flag)
            def _():
                row_copy(step, way).wait_send()

    obs1_moved().wait_send()

    @pl.when(inner)
    def _():
        obs3_copy().wait_send()

    @pl.when(outer)
    def _():
        late_copy().wait_send()


def steps(*operands):
    dma = pltpu.SemaphoreType.DMA
    state = (FIELDS, ROWS, COLS)
    terms = 2 * POINTS * EDGE
    pairs = LINES // 2
    inputs = [
        pltpu.SMEM(x.shape, x.dtype) if i in (2, 3) else pltpu.VMEM(x.shape, x.dtype)
        for i, x in enumerate(operands)
    ]
    return pl.pallas_call(
        kernel,
        out_shape=pltpu.VMEM(state, F32),
        in_specs=[pl.BlockSpec(memory_space=pltpu.HBM)] * len(operands),
        out_specs=pl.BlockSpec(memory_space=pltpu.VMEM),
        scratch_shapes=inputs + [
            dma((len(operands),)),
            pltpu.VMEM(state, F32),
            pltpu.VMEM(state, F32),
            pltpu.VMEM(state[1:], F32),
            pltpu.VMEM(state, F32),
            pltpu.VMEM((2, 2) + state, F32),
            pltpu.VMEM((2, 2, FIELDS, COLS), F32),
            pltpu.VMEM((2, 2, FIELDS, COLS), F32),
            pltpu.VMEM((2, 1, LANES), F32),
            pltpu.VMEM((2, TILES, LANES), F32),
            pltpu.VMEM((2, 8, EDGE), F32),
            pltpu.VMEM((HIGH, terms), BF16),
            pltpu.VMEM((WIDE, terms), BF16),
            pltpu.VMEM((2 * FIELDS * HIGH, terms), BF16),
            pltpu.VMEM((TILES, 4, LANES), F32),
            pltpu.VMEM((TILES, 4, LANES), F32),
            pltpu.VMEM((GROUP, pairs, 4, LANES), F32),
            pltpu.VMEM((LAYERS, GROUP, pairs, 4, LANES), F32),
            pltpu.VMEM((2 * HIGH, WIDE), F32),
            pltpu.VMEM(state[1:], F32),
            pltpu.VMEM(state[1:], F32),
            dma((2, 2)), dma((2, 2, len(PIECES))),
            dma((2, 2)), dma((2, 2)),
            dma((2,)), dma((2,)),
            dma((3,)), dma((4,)),
            dma(()), dma(()), pltpu.SemaphoreType.REGULAR,
        ],
        compiler_params=pltpu.CompilerParams(
            collective_id=0, has_side_effects=True, vmem_limit_bytes=61440 << 10
        ),
        name="adjoint_steps",
    )(*operands)


def body(
    adj_final, cond, diffus, couple, ghost_row, ghost_col, ghost_wt, obs_dest, obs_cell, obs_wt,
    misfit,
):
    final = steps(
        adj_final.reshape(FIELDS, ROWS, COLS), cond[0, 0], diffus, couple, ghost_row, ghost_col,
        ghost_wt, obs_dest.reshape(1, OBS), obs_cell[0, 0], obs_wt[0, 0], misfit[0, 0],
    )
    return final[None, :, None]


def solution(mesh):
    placed = (
        P("panel", None, "rad", "ang", None),
        P("panel", "rad", "ang", None),
        P(),
        P(),
        P(),
        P(),
        P(),
        P("panel", "rad", "ang", None),
        P("panel", "rad", None, "ang"),
        P("panel", "rad", None, "ang"),
        P("panel", "rad", None, "ang"),
    )
    return jax.shard_map(
        body,
        mesh=mesh,
        in_specs=placed,
        out_specs=P("panel", None, "rad", "ang", None),
        check_vma=False,
    )
```

```python
import functools
import jax
import jax.numpy as jnp
from jax import lax
from jax.experimental import pallas as pl
from jax.experimental.pallas import tpu as pltpu
from jax.sharding import PartitionSpec as P

MESH = pl.DeviceIdType.MESH
F32, BF16 = jnp.float32, jnp.bfloat16
FIELDS, ROWS, COLS = 7, 8, 1536
LANES = 128
BLOCKS = COLS // LANES
WIDE = 256
SPANS = COLS // WIDE
HIGH = ROWS * SPANS
LAYERS, TILES, GROUP = 8, 32, 4
LINES = TILES // GROUP
HALF = LAYERS // 2
SLOTS = 16
POINTS = 4
OBS = 256
EDGE = TILES * ROWS
FORCED = 3

PIECES = ((0, 128), (1408, 1536), (128, 768), (768, 1408))
EDGE_PIECES = 2


def iota(shape, dim, dtype=jnp.int32):
    value = lax.broadcasted_iota(jnp.int32, shape, dim)
    return value if dtype == jnp.int32 else value.astype(dtype)


def dot_rows(a, b, precision=None):
    return lax.dot_general(
        a, b, (((1,), (1,)), ((), ())), precision=precision, preferred_element_type=F32
    )


def indicator(count, row):
    small = row.astype(BF16)
    hot = iota((count, row.shape[1]), 0, F32).astype(BF16) == jnp.broadcast_to(small, (count, row.shape[1]))
    return jnp.where(hot, jnp.ones((), BF16), jnp.zeros((), BF16))


def spread(high_hot, row):
    count, width = high_hot.shape
    wide = jnp.broadcast_to(row, (16, width))
    top = wide.astype(BF16)
    rest = (wide - top.astype(F32)).astype(BF16)
    grid = high_hot.reshape(count // 16, 16, width)
    return [(grid * part[None]).reshape(count, width) for part in (top, rest)]


def kernel(
    adj_hbm, cond_hbm, diffus_hbm, couple_hbm, ghost_row_hbm, ghost_col_hbm, ghost_wt_hbm,
    dest_hbm, cell_hbm, obs_wt_hbm, misfit_hbm,
    out,
    adj, cond, diffus, couple, ghost_row, ghost_col, ghost_wt, dest, cell, obs_wt, misfit, load_s,
    scaled_a, scaled_b, scaled_f, base, layer_in, row_out, row_in,
    edge_out, edge_all, edge_rows,
    high_hot, low_hot, spread_rows,
    outbox, line_in, pair_sum, tile_in, forced_in, forcing, late_out, late_in,
    layer_ss, layer_rs, row_ss, row_rs,
    edge_ss, edge_rs, obs_ss, obs_rs, late_ss, late_rs, open_s,
):
    loads = [
        pltpu.make_async_copy(source, target, load_s.at[i])
        for i, (source, target) in enumerate((
            (adj_hbm, adj), (cond_hbm, cond), (diffus_hbm, diffus), (couple_hbm, couple),
            (dest_hbm, dest), (cell_hbm, cell), (obs_wt_hbm, obs_wt), (misfit_hbm, misfit),
            (ghost_row_hbm, ghost_row), (ghost_col_hbm, ghost_col), (ghost_wt_hbm, ghost_wt),
        ))
    ]
    for load in loads[:3]:
        load.start()

    p, z, a = lax.axis_index("panel"), lax.axis_index("rad"), lax.axis_index("ang")
    y, q = a // GROUP, lax.rem(a, GROUP)
    has_low, has_high = z > 0, z < LAYERS - 1
    has_north, has_south = a > 0, a < TILES - 1
    outer = z == LAYERS - 1
    inner = z < LAYERS - 1
    scaled = (scaled_a, scaled_b)

    def along_line(step):
        return lax.rem(y + step, LINES)

    def beside(step):
        return lax.rem(q + step, GROUP)

    barrier = pltpu.get_barrier_semaphore()

    def greet(panel, layer, tile):
        pl.semaphore_signal(barrier, inc=1, device_id=(panel, layer, tile), device_id_type=MESH)

    order = sorted(range(TILES), key=lambda i: -min(i, TILES - i))
    for i in order:
        greet(1 - p, z, lax.rem(a + i, TILES))
    for i in sorted(range(1, LINES), key=lambda i: -min(i, LINES - i)):
        greet(p, z, along_line(i) * GROUP + q)

    @pl.when(has_low)
    def _():
        greet(p, z - 1, a)

    @pl.when(has_high)
    def _():
        greet(p, z + 1, a)

    @pl.when(has_north)
    def _():
        greet(p, z, a - 1)

    @pl.when(has_south)
    def _():
        greet(p, z, a + 1)

    for i in range(1, GROUP):
        greet(p, z, y * GROUP + beside(i))

    @pl.when(inner)
    def _():
        greet(p, LAYERS - 1, a)

    for load in loads[3:]:
        load.start()

    def remote(source, target, send, recv, device):
        return pltpu.make_async_remote_copy(
            src_ref=source, dst_ref=target, send_sem=send, recv_sem=recv,
            device_id=device, device_id_type=MESH,
        )

    def layer_copy(step, way, start=0, stop=COLS, piece=0):
        return remote(
            scaled[step].at[:, :, start:stop], layer_in.at[step, way, :, :, start:stop],
            layer_ss.at[step, way], layer_rs.at[step, way, piece],
            (p, z + 1 if way == 0 else z - 1, a),
        )

    def row_copy(step, way):
        return remote(
            row_out.at[step, way], row_in.at[step, way], row_ss.at[step, way], row_rs.at[step, way],
            (p, z, a + 1 if way == 0 else a - 1),
        )

    def edge_copy(step, i):
        return remote(
            edge_out.at[step], edge_all.at[step, pl.ds(a, 1), :], edge_ss.at[step], edge_rs.at[step],
            (1 - p, z, lax.rem(a + i, TILES)),
        )

    def edges_moved(step):
        everything = edge_all.at[step]
        return remote(everything, everything, edge_ss.at[step], edge_rs.at[step], (1 - p, z, a))

    def obs1_copy(i):
        target = along_line(i)
        return remote(
            outbox.at[pl.ds(target * GROUP, GROUP)], line_in.at[y], obs_ss.at[0], obs_rs.at[0],
            (p, z, target * GROUP + q),
        )

    def obs1_moved():
        others = line_in.at[pl.ds(0, LINES - 1)]
        return remote(others, others, obs_ss.at[0], obs_rs.at[0], (1 - p, z, a))

    def obs2_copy(i):
        target = beside(i)
        return remote(
            pair_sum.at[target], tile_in.at[q], obs_ss.at[1], obs_rs.at[1],
            (p, z, y * GROUP + target),
        )

    def obs2_moved():
        others = tile_in.at[pl.ds(0, GROUP - 1)]
        return remote(others, others, obs_ss.at[1], obs_rs.at[1], (1 - p, z, a))

    def obs3_copy():
        return remote(
            tile_in, forced_in.at[z], obs_ss.at[2], obs_rs.at[2 + z // HALF], (p, LAYERS - 1, a)
        )

    def obs3_moved(start, count):
        others = forced_in.at[pl.ds(start, count)]
        return remote(
            others, others, obs_ss.at[2], obs_rs.at[2 + start // HALF], (1 - p, z, a)
        )

    def late_copy():
        return remote(late_out, late_in, late_ss, late_rs, (p, z - 1, a))

    def send_layers(step, piece):
        start, stop = PIECES[piece]

        @pl.when(has_high)
        def _():
            layer_copy(step, 0, start, stop, piece).start()

        @pl.when(has_low)
        def _():
            layer_copy(step, 1, start, stop, piece).start()

    def take_layers(step, piece):
        start, stop = PIECES[piece]

        @pl.when(has_low)
        def _():
            layer_copy(step, 0, start, stop, piece).wait_recv()

        @pl.when(has_high)
        def _():
            layer_copy(step, 1, start, stop, piece).wait_recv()

    def send_rows(step):
        @pl.when(has_south)
        def _():
            row_copy(step, 0).start()

        @pl.when(has_north)
        def _():
            row_copy(step, 1).start()

    def take_rows(step):
        @pl.when(has_north)
        def _():
            row_copy(step, 0).wait_recv()

        @pl.when(has_south)
        def _():
            row_copy(step, 1).wait_recv()

    def field_of(step, f):
        return scaled_f if step == 1 and f == FORCED else scaled[step].at[f]

    runs = LANES // ROWS
    lane_of = iota((ROWS, LANES), 1)
    own_run = jnp.where(
        lax.rem(lane_of, ROWS) == iota((ROWS, LANES), 0),
        lax.rem(lane_of // ROWS - lax.rem(a, runs) + runs, runs), -1,
    )
    sent_run = lax.rem(iota((runs, LANES), 1) // ROWS - iota((runs, LANES), 0) + runs, runs)

    def fill_rows(step):
        for f in range(FIELDS):
            row_out[step, 0, f:f + 1, :] = field_of(step, f)[ROWS - 1:ROWS, :]
            row_out[step, 1, f:f + 1, :] = field_of(step, f)[0:1, :]

    def fill_edges(step):
        wide = jnp.zeros((ROWS, LANES), F32)
        for f in range(FIELDS):
            for side, at in ((0, 0), (1, COLS - 1)):
                start = at // LANES * LANES
                block = field_of(step, f)[:, start:start + LANES]
                column = block[:, at - start:at - start + 1]
                wide = jnp.where(
                    own_run == 2 * f + side, jnp.broadcast_to(column, (ROWS, LANES)), wide
                )
        edge_out[step] = jnp.sum(wide, axis=0, keepdims=True)

    def send_edges(step):
        fill_edges(step)
        for i in order:
            edge_copy(step, i).start()

    def fill_base(step, source, target):
        rate = [[couple[e, c] for c in range(FIELDS)] for e in range(FIELDS)]
        for b in range(BLOCKS):
            cols = slice(b * LANES, (b + 1) * LANES)
            state = [source[e, :, cols] for e in range(FIELDS)]
            for c in range(FIELDS):
                total = state[c]
                for e in range(FIELDS):
                    total = total + rate[e][c] * state[e]
                target[c, :, cols] = total
        col_of = iota((ROWS, COLS), 1)
        row_of = iota((ROWS, COLS), 0)
        for f in range(FIELDS):
            s = field_of(step, f)[...]
            west = jnp.where(col_of == 0, 0.0, pltpu.roll(s, 1, 1))
            east = jnp.where(col_of == COLS - 1, 0.0, pltpu.roll(s, COLS - 1, 1))
            north = jnp.where(row_of == 0, 0.0, pltpu.roll(s, 1, 0))
            south = jnp.where(row_of == ROWS - 1, 0.0, pltpu.roll(s, ROWS - 1, 0))
            target[f] = target[f] + ((west + east) + (north + south) - 6.0 * s)

    def add_ghost(step, target):
        edges_moved(step).wait_recv()
        for f in range(FIELDS):
            for side in range(2):
                run = 2 * f + side
                for h in range(2):
                    part = jnp.where(
                        sent_run == run, edge_all[step, h * runs:(h + 1) * runs, :], 0.0
                    )
                    line = jnp.sum(part, axis=0, keepdims=True)
                    if run:
                        line = pltpu.roll(line, LANES - ROWS * run, 1)
                    edge_rows[side, f:f + 1, h * LANES:(h + 1) * LANES] = line
        for f in range(FIELDS):
            rows = [
                edge_rows[side, f:f + 1, :] * ghost_wt[side, point:point + 1, :]
                for side in range(2) for point in range(POINTS)
            ]
            top, rest = spread(high_hot[...], jnp.concatenate(rows, axis=1))
            spread_rows[f * HIGH:(f + 1) * HIGH] = top
            spread_rows[(FIELDS + f) * HIGH:(FIELDS + f + 1) * HIGH] = rest
        cells = dot_rows(spread_rows[...], low_hot[...])
        for f in range(FIELDS):
            for b in range(SPANS):
                at = f * HIGH + b * ROWS
                more = at + FIELDS * HIGH
                cols = slice(b * WIDE, (b + 1) * WIDE)
                target[f, :, cols] = target[f, :, cols] + (
                    cells[at:at + ROWS] + cells[more:more + ROWS]
                )

    for load in loads[:3]:
        load.wait()
    for f in range(FIELDS):
        scaled_a[f] = (diffus[f] * cond[...]) * adj[f]

    fill_edges(0)
    fill_rows(0)

    for load in loads[3:]:
        load.wait()
    owner_hot = jnp.where(iota((TILES, OBS), 0) == dest[...], 1.0, 0.0)
    earlier = jnp.where(iota((OBS, OBS), 1) < iota((OBS, OBS), 0), 1.0, 0.0).astype(BF16)
    before = dot_rows(owner_hot.astype(BF16), earlier)
    rank = jnp.sum(owner_hot * before, axis=0, keepdims=True)
    in_slot = rank == iota((SLOTS, OBS), 0, F32)
    number = cell[...]
    in_row = jnp.floor((number.astype(F32) + 0.5) * (1.0 / COLS)).astype(jnp.int32)
    column = number - in_row * COLS
    place = (
        (lax.shift_right_logical(column, 8) * ROWS + in_row) * WIDE + (column & (WIDE - 1))
    ).astype(F32)
    payload = []
    for kind in range(3):
        for point in range(POINTS):
            if kind < 2:
                row = misfit[kind:kind + 1, :] * obs_wt[point:point + 1, :]
            else:
                row = place[point:point + 1, :]
            payload.append(jnp.where(in_slot, jnp.broadcast_to(row, (SLOTS, OBS)), 0.0))
    packed = dot_rows(owner_hot, jnp.concatenate(payload, axis=0), lax.Precision.HIGHEST)
    width = SLOTS * POINTS
    own_half = iota((TILES, LANES), 1) // width == lax.rem(y, 2)
    for kind in range(3):
        part = packed[:, kind * width:(kind + 1) * width]
        outbox[:, kind, :] = jnp.where(own_half, jnp.concatenate([part, part], axis=1), 0.0)
    outbox[:, 3, :] = jnp.zeros((TILES, LANES), F32)
    for side in range(2):
        for point in range(POINTS):
            at = (side * POINTS + point) * EDGE
            local = ghost_row[side, point:point + 1, :] - a * ROWS
            col = ghost_col[side, point:point + 1, :]
            inside = (local >= 0) & (local < ROWS)
            high = jnp.where(inside, lax.shift_right_logical(col, 8) * ROWS + local, -1)
            low = col & (WIDE - 1)
            high_hot[:, at:at + EDGE] = indicator(HIGH, high.astype(F32))
            low_hot[:, at:at + EDGE] = indicator(WIDE, low.astype(F32))

    def count(flag):
        return jnp.where(flag, 1, 0)

    expected = (
        TILES + LINES - 1 + GROUP - 1
        + count(has_low) + count(has_high) + count(has_north) + count(has_south)
        + jnp.where(outer, LAYERS - 1, 0)
    )
    pl.semaphore_wait(barrier, expected)

    @pl.when(outer)
    def _():
        for i in range(LAYERS - 1):
            pl.semaphore_signal(open_s, inc=1, device_id=(p, i, a), device_id_type=MESH)

    for i in range(1, LINES):
        obs1_copy(i).start()
    line_in[y] = outbox[pl.ds(y * GROUP, GROUP)]

    for i in order:
        edge_copy(0, i).start()
    for piece in range(len(PIECES)):
        send_layers(0, piece)
    send_rows(0)

    obs1_moved().wait_recv()
    for i in range(GROUP):
        for pair in range(LINES // 2):
            pair_sum[i, pair] = line_in[2 * pair, i] + line_in[2 * pair + 1, i]
    for i in range(1, GROUP):
        obs2_copy(i).start()
    tile_in[q] = pair_sum[q]

    for step in range(2):
        @pl.when(jnp.logical_not(has_low))
        def _():
            layer_in[step, 0] = jnp.zeros((FIELDS, ROWS, COLS), F32)

        @pl.when(jnp.logical_not(has_high))
        def _():
            layer_in[step, 1] = jnp.zeros((FIELDS, ROWS, COLS), F32)

        @pl.when(jnp.logical_not(has_north))
        def _():
            row_in[step, 0] = jnp.zeros((FIELDS, COLS), F32)

        @pl.when(jnp.logical_not(has_south))
        def _():
            row_in[step, 1] = jnp.zeros((FIELDS, COLS), F32)

    fill_base(0, adj, base)
    obs2_moved().wait_recv()

    def send_third(flag):
        @pl.when(flag)
        def _():
            pl.semaphore_wait(open_s, 1)
            obs3_copy().start()

    send_third(inner & (z >= 2))

    add_ghost(0, base)

    def one_layer(layer, carry):
        rows = [[], [], []]
        for i in range(GROUP):
            for pair in range(LINES // 2):
                for kind in range(3):
                    rows[kind].append(forced_in[layer, i, pair, kind:kind + 1, :])
        early, late, places = [jnp.concatenate(r, axis=1) for r in rows]
        high = jnp.floor(places * (1.0 / WIDE))
        hot_high = indicator(HIGH, high)
        hot_low = indicator(WIDE, places - high * WIDE)
        top_a, rest_a = spread(hot_high, early)
        top_b, rest_b = spread(hot_high, late)
        cells = dot_rows(jnp.concatenate([top_a, top_b, rest_a, rest_b], axis=0), hot_low)
        forcing[...] = forcing[...] + (cells[:2 * HIGH] + cells[2 * HIGH:])
        return carry

    @pl.when(outer)
    def _():
        forcing[...] = jnp.zeros((2 * HIGH, WIDE), F32)
        obs3_moved(0, HALF).wait_recv()
        lax.fori_loop(0, HALF, one_layer, 0, unroll=2)

    def with_halos(value, step, f, start, stop):
        size = stop - start
        row_of = iota((ROWS, size), 0)
        value = value + (layer_in[step, 0, f, :, start:stop] + layer_in[step, 1, f, :, start:stop])
        north = jnp.broadcast_to(row_in[step, 0, f:f + 1, start:stop], (ROWS, size))
        south = jnp.broadcast_to(row_in[step, 1, f:f + 1, start:stop], (ROWS, size))
        return value + jnp.where(row_of == 0, north, jnp.where(row_of == ROWS - 1, south, 0.0))

    take_rows(0)
    for piece, (start, stop) in enumerate(PIECES):
        take_layers(0, piece)
        for f in range(FIELDS):
            value = with_halos(base[f, :, start:stop], 0, f, start, stop)
            base[f, :, start:stop] = value
            scaled_b[f, :, start:stop] = (diffus[f] * cond[:, start:stop]) * value
        send_layers(1, piece)
        if piece == EDGE_PIECES - 1:
            scaled_f[:, :LANES] = scaled_b[FORCED, :, :LANES]
            scaled_f[:, COLS - LANES:] = scaled_b[FORCED, :, COLS - LANES:]

            @pl.when(inner)
            def _():
                send_edges(1)

            send_third(z < 2)
    scaled_f[...] = scaled_b[FORCED]

    @pl.when(outer)
    def _():
        forced_in[LAYERS - 1] = tile_in[...]
        obs3_moved(HALF, HALF - 1).wait_recv()
        lax.fori_loop(HALF, LAYERS, one_layer, 0, unroll=2)
        for b in range(SPANS):
            cols = slice(b * WIDE, (b + 1) * WIDE)
            added = forcing[HIGH + b * ROWS:HIGH + (b + 1) * ROWS]
            share = (diffus[FORCED] * cond[:, cols]) * added
            base[FORCED, :, cols] = base[FORCED, :, cols] + added
            scaled_f[:, cols] = scaled_f[:, cols] + share
            late_out[:, cols] = share
        send_edges(1)
        late_copy().start()

    fill_rows(1)
    send_rows(1)

    fill_base(1, base, out)

    def finish(piece):
        start, stop = PIECES[piece]
        take_layers(1, piece)
        for f in range(FIELDS):
            out[f, :, start:stop] = with_halos(out[f, :, start:stop], 1, f, start, stop)

    take_rows(1)
    for piece in range(len(PIECES) - 1):
        finish(piece)
    add_ghost(1, out)

    @pl.when(outer)
    def _():
        for b in range(SPANS):
            cols = slice(b * WIDE, (b + 1) * WIDE)
            out[FORCED, :, cols] = out[FORCED, :, cols] + forcing[b * ROWS:(b + 1) * ROWS]

    finish(len(PIECES) - 1)

    @pl.when(z == LAYERS - 2)
    def _():
        late_copy().wait_recv()
        out[FORCED] = out[FORCED] + late_in[...]

    for step in range(2):
        edges_moved(step).wait_send()
        for way, flag in ((0, has_high), (1, has_low)):
            @pl.when(flag)
            def _():
                layer_copy(step, way).wait_send()

        for way, flag in ((0, has_south), (1, has_north)):
            @pl.when(flag)
            def _():
                row_copy(step, way).wait_send()

    obs1_moved().wait_send()
    obs2_moved().wait_send()

    @pl.when(inner)
    def _():
        obs3_copy().wait_send()

    @pl.when(outer)
    def _():
        late_copy().wait_send()


def steps(*operands):
    dma = pltpu.SemaphoreType.DMA
    state = (FIELDS, ROWS, COLS)
    terms = 2 * POINTS * EDGE
    pairs = LINES // 2
    inputs = [
        pltpu.SMEM(x.shape, x.dtype) if i in (2, 3) else pltpu.VMEM(x.shape, x.dtype)
        for i, x in enumerate(operands)
    ]
    return pl.pallas_call(
        kernel,
        out_shape=pltpu.VMEM(state, F32),
        in_specs=[pl.BlockSpec(memory_space=pltpu.HBM)] * len(operands),
        out_specs=pl.BlockSpec(memory_space=pltpu.VMEM),
        scratch_shapes=inputs + [
            dma((len(operands),)),
            pltpu.VMEM(state, F32),
            pltpu.VMEM(state, F32),
            pltpu.VMEM(state[1:], F32),
            pltpu.VMEM(state, F32),
            pltpu.VMEM((2, 2) + state, F32),
            pltpu.VMEM((2, 2, FIELDS, COLS), F32),
            pltpu.VMEM((2, 2, FIELDS, COLS), F32),
            pltpu.VMEM((2, 1, LANES), F32),
            pltpu.VMEM((2, TILES, LANES), F32),
            pltpu.VMEM((2, 8, EDGE), F32),
            pltpu.VMEM((HIGH, terms), BF16),
            pltpu.VMEM((WIDE, terms), BF16),
            pltpu.VMEM((2 * FIELDS * HIGH, terms), BF16),
            pltpu.VMEM((TILES, 4, LANES), F32),
            pltpu.VMEM((LINES, GROUP, 4, LANES), F32),
            pltpu.VMEM((GROUP, pairs, 4, LANES), F32),
            pltpu.VMEM((GROUP, pairs, 4, LANES), F32),
            pltpu.VMEM((LAYERS, GROUP, pairs, 4, LANES), F32),
            pltpu.VMEM((2 * HIGH, WIDE), F32),
            pltpu.VMEM(state[1:], F32),
            pltpu.VMEM(state[1:], F32),
            dma((2, 2)), dma((2, 2, len(PIECES))),
            dma((2, 2)), dma((2, 2)),
            dma((2,)), dma((2,)),
            dma((3,)), dma((4,)),
            dma(()), dma(()), pltpu.SemaphoreType.REGULAR,
        ],
        compiler_params=pltpu.CompilerParams(
            collective_id=0, has_side_effects=True, vmem_limit_bytes=61440 << 10
        ),
        name="adjoint_steps",
    )(*operands)


def body(
    adj_final, cond, diffus, couple, ghost_row, ghost_col, ghost_wt, obs_dest, obs_cell, obs_wt,
    misfit,
):
    final = steps(
        adj_final.reshape(FIELDS, ROWS, COLS), cond[0, 0], diffus, couple, ghost_row, ghost_col,
        ghost_wt, obs_dest.reshape(1, OBS), obs_cell[0, 0], obs_wt[0, 0], misfit[0, 0],
    )
    return final[None, :, None]


def solution(mesh):
    placed = (
        P("panel", None, "rad", "ang", None),
        P("panel", "rad", "ang", None),
        P(),
        P(),
        P(),
        P(),
        P(),
        P("panel", "rad", "ang", None),
        P("panel", "rad", None, "ang"),
        P("panel", "rad", None, "ang"),
        P("panel", "rad", None, "ang"),
    )
    return jax.shard_map(
        body,
        mesh=mesh,
        in_specs=placed,
        out_specs=P("panel", None, "rad", "ang", None),
        check_vma=False,
    )
```
